128 devices in a mesh: box: 32 (over x, z, core), dir: 4 (over y).
Axes of the slice: x: 4, y: 4, z: 4, core: 2. Of those that a mesh axis runs over, the one named last changes fastest.
Arguments:
- child_pat: bfloat16 [4096, 2, 8, 2048], P('box', None, None, 'dir'), may hold values from -6 to 6
- interp: bfloat16 [64, 4, 128, 128], P('dir'), may hold values from -0.25 to 0.25
- interp_blocks: int32 [64, 4], P('dir'), may hold values from 0 to 15, as said below
- shift_angle: float32 [8, 8192], P(None, 'dir'), may hold values from -3.140625 to 3.140625
- slot_parent: int32 [512], replicated, may hold values from 0 to 511, each once
- far_list: int32 [512, 189], replicated, may hold values from -1 to 511, as said below
- trans: float32 [2, 343, 8192], P(None, None, 'dir'), may hold values from -0.15625 to 0.15625
Outputs:
- far_field: float32 [512, 2, 8, 8192], P('box', None, None, 'dir')
The draws below stay inside these ranges and needn't reach their ends.
Inputs may be any that keep to these rules, and one draw needn't show every extreme that they name: `interp_blocks`: entry (j, b) is (j * 16 // 64 + o) modulo 16, for four different o of -2 to 2 in increasing order. `far_list`: row p lists, in increasing order of code(p, q), the occupied parents q whose own parents are neighbours of p's parent (coordinates differ by at most one) and that are not neighbours of p, then -1 to the end; each coordinate of q - p lies within -3 to 3; some row lists 189 partners.
All inputs are finite; a program needn't handle non-finite values.
Results may differ from the reference program's by a relative error of at most 0.0029.
Values may be sent and summed in bfloat16 or wider, within the bound.
A program may use at most 192 MiB of HBM per device.

```python
import jax
import jax.numpy as jnp
from jax import lax

G = 8
PARENTS = 512
CHILD = 4096
K1 = 2048
K2 = 8192
BS = 128
NB = 4
NBI = 16
NBO = 64
FAR = 189
OFFS = 343
R = 8


def draw_interp_blocks(key, part):
    drop = jax.random.randint(jax.random.fold_in(key, 7), (NBO, 1), 0, 5)
    steps = jnp.arange(NB, dtype=jnp.int32)[None, :]
    offset = jnp.where(steps >= drop, steps + 1, steps) - 2
    center = (jnp.arange(NBO, dtype=jnp.int32) * NBI // NBO)[:, None]
    return ((center + offset) % NBI).astype(jnp.int32)


def draw_far_list(key, part):
    ident = jnp.arange(PARENTS, dtype=jnp.int32)
    pos_x = ident // (G * G)
    pos_y = ident // G % G
    pos_z = ident % G
    center = jax.random.randint(jax.random.fold_in(key, 12), (3,), 1, G // 2 - 1)
    lower = 2 * center - 2
    upper = 2 * center + 3
    inside = (pos_x >= lower[0]) & (pos_x <= upper[0]) & (pos_y >= lower[1]) & (pos_y <= upper[1]) & (pos_z >= lower[2]) & (pos_z <= upper[2])
    filled = (jax.random.randint(jax.random.fold_in(key, 11), (PARENTS,), 0, 10) < 7) | inside
    codes = jnp.arange(343, dtype=jnp.int32)
    off_x = codes // 49 - 3
    off_y = codes // 7 % 7 - 3
    off_z = codes % 7 - 3
    tgt_x = pos_x[:, None] + off_x[None, :]
    tgt_y = pos_y[:, None] + off_y[None, :]
    tgt_z = pos_z[:, None] + off_z[None, :]
    in_grid = (tgt_x >= 0) & (tgt_x < G) & (tgt_y >= 0) & (tgt_y < G) & (tgt_z >= 0) & (tgt_z < G)
    grand_ok = (jnp.abs(tgt_x // 2 - pos_x[:, None] // 2) <= 1) & (jnp.abs(tgt_y // 2 - pos_y[:, None] // 2) <= 1) & (jnp.abs(tgt_z // 2 - pos_z[:, None] // 2) <= 1)
    reach = jnp.maximum(jnp.maximum(jnp.abs(off_x), jnp.abs(off_y)), jnp.abs(off_z))
    not_near = (reach >= 2)[None, :]
    target = jnp.where(in_grid, tgt_x * G * G + tgt_y * G + tgt_z, 0)
    valid = in_grid & grand_ok & not_near & filled[target]
    sort_key = jnp.where(valid, codes[None, :], 343 + codes[None, :])
    order = jnp.argsort(sort_key, axis=1)[:, :FAR]
    chosen_valid = jnp.take_along_axis(valid, order, axis=1)
    chosen = jnp.take_along_axis(target, order, axis=1)
    return jnp.where(chosen_valid, chosen, -1).astype(jnp.int32)


def levels(stream_key, shape, cuts, smallest, largest):
    level, own = 1.0, jax.random.fold_in(stream_key, 6)
    for dim, shards_of in cuts:
        steps = jnp.exp(jax.random.uniform(jax.random.fold_in(own, dim), (shards_of,), jnp.float32, smallest / len(cuts), largest / len(cuts)))
        level = level * jnp.repeat(steps, shape[dim] // shards_of).reshape([-1 if axis == dim else 1 for axis in range(len(shape))])
    return level


def normal_values(own_key, shape, spread, most, pieces=(), kind=jnp.bfloat16):
    loudness = levels(own_key, shape, pieces, -0.22, 0.18) if pieces else 1.0
    entries = jax.random.normal(own_key, shape, jnp.float32) * spread * loudness
    return jnp.minimum(jnp.maximum(entries, -most), most).astype(kind)


def setup_inputs(seed: int = 0) -> dict:
    streams_of = jax.random.split(jax.random.key(seed), 8)
    child_pat = normal_values(streams_of[0], (CHILD, 2, R, K1), 1.0, 6.0, ((0, 32), (3, 4)))
    interp = normal_values(streams_of[1], (NBO, NB, BS, BS), (NB * BS) ** -0.5, 0.25, ((0, 4),))
    interp_blocks = draw_interp_blocks(jax.random.fold_in(streams_of[7], 71), 0)
    shift_angle = jnp.clip(jax.random.uniform(streams_of[3], (8, K2), jnp.float32, -3.140625, 3.140625), -3.140625, 3.140625)
    slot_parent = jax.random.permutation(streams_of[4], PARENTS).astype(jnp.int32)
    far_list = draw_far_list(jax.random.fold_in(streams_of[7], 71), 0)
    trans = normal_values(streams_of[6], (2, OFFS, K2), (8 * FAR) ** -0.5, 0.15625, ((2, 4),), jnp.float32)
    return dict(child_pat=child_pat, interp=interp, interp_blocks=interp_blocks, shift_angle=shift_angle, slot_parent=slot_parent, far_list=far_list, trans=trans)


def translate(patterns, table, slot_parent, slot_of, far_list, targets):
    parent = slot_parent[targets]
    listed = far_list[parent]
    valid = listed >= 0
    partner = jnp.where(valid, listed, 0)
    source = slot_of[partner]
    pos_x = (parent // (G * G))[:, None]
    pos_y = ((parent // G) % G)[:, None]
    pos_z = (parent % G)[:, None]
    code = (partner // (G * G) - pos_x + 3) * 49 + ((partner // G) % G - pos_y + 3) * 7 + (partner % G - pos_z + 3)
    code = jnp.where(valid, code, 0)
    mask = valid.astype(jnp.float32)[:, :, None]
    real_tab = (table[0][code] * mask)[:, :, None, :]
    imag_tab = (table[1][code] * mask)[:, :, None, :]
    rows = patterns[source].astype(jnp.float32)
    out_real = jnp.sum(real_tab * rows[:, :, 0] - imag_tab * rows[:, :, 1], axis=1)
    out_imag = jnp.sum(real_tab * rows[:, :, 1] + imag_tab * rows[:, :, 0], axis=1)
    return jnp.stack([out_real, out_imag], axis=1)


def reference(child_pat, interp, interp_blocks, shift_angle, slot_parent, far_list, trans):
    def one_block(index):
        blocks = interp_blocks[index]
        total = jnp.zeros((CHILD * 2 * R, BS), jnp.float32)
        for part in range(NB):
            start = (blocks[part] * BS).astype(jnp.int32)
            piece = lax.dynamic_slice_in_dim(child_pat, start, BS, 3).reshape(CHILD * 2 * R, BS)
            total = total + jnp.dot(piece, interp[index, part], preferred_element_type=jnp.float32)
        upsampled = total.reshape(PARENTS, 8, 2, R, BS)
        angle = lax.dynamic_slice_in_dim(shift_angle, (index * BS).astype(jnp.int32), BS, 1)
        cosine = jnp.cos(angle)[None, :, None, :]
        sine = jnp.sin(angle)[None, :, None, :]
        real_part = upsampled[:, :, 0]
        imag_part = upsampled[:, :, 1]
        out_real = jnp.sum(cosine * real_part - sine * imag_part, axis=1)
        out_imag = jnp.sum(sine * real_part + cosine * imag_part, axis=1)
        return jnp.stack([out_real, out_imag], axis=1).astype(jnp.bfloat16)

    blocks_out = lax.map(one_block, jnp.arange(NBO, dtype=jnp.int32))
    parent_pat = jnp.transpose(blocks_out, (1, 2, 3, 0, 4)).reshape(PARENTS, 2, R, K2)
    slot_of = jnp.zeros((PARENTS,), jnp.int32).at[slot_parent].set(jnp.arange(PARENTS, dtype=jnp.int32))

    def one_slot(target):
        return translate(parent_pat, trans, slot_parent, slot_of, far_list, target[None])[0]

    return lax.map(one_slot, jnp.arange(PARENTS, dtype=jnp.int32))
```

```python
import jax
import jax.numpy as jnp
from jax import lax
from jax.experimental import pallas as pl
from jax.experimental.pallas import tpu as pltpu
from jax.sharding import PartitionSpec as P

G = 8
F1 = 18
NF = F1 * F1


def toom_in(v):
    a, b = v[0] + v[2], v[1] + v[3]
    c, d = v[0] + 4.0 * v[2], 2.0 * v[1] + 8.0 * v[3]
    return [v[0], v[3], a + b, a - b, c + d, c - d]


def line_in(x):
    even, odd = x[0::2], x[1::2]
    both = [e + o for e, o in zip(even, odd)]
    return toom_in(both) + toom_in(odd) + toom_in(even)


def toom_kernel(k):
    h2, h1, h0 = k
    a, b = (h0 + h2) * 0.5, h1 * 0.5
    c, d = (h0 + 4.0 * h2) * (1.0 / 24.0), h1 * (1.0 / 12.0)
    return [h0, h2, a + b, a - b, c + d, c - d]


def line_kernel(t):
    k0 = [t[1], t[3], t[5]]
    up = [t[2] - t[1], t[4] - t[3], t[6] - t[5]]
    down = [t[0] - t[1], t[2] - t[3], t[4] - t[5]]
    return toom_kernel(k0) + toom_kernel(up) + toom_kernel(down)


def toom_out(m):
    z0, z5 = m[0], m[1]
    e1, o1 = m[2] + m[3], m[2] - m[3]
    e2, d2 = m[4] + m[5], m[4] - m[5]
    z4 = e2 - e1 * (1.0 / 3.0) + z0 * 0.25
    z2 = e1 - z0 - z4
    z3 = 2.0 * d2 - o1 * (1.0 / 3.0) - 5.0 * z5
    z1 = o1 - z3 - z5
    return [z1, z2, z3, z4]


def line_out(m):
    base, up, down = toom_out(m[0:6]), toom_out(m[6:12]), toom_out(m[12:18])
    out = []
    for i in range(4):
        out += [base[i] + up[i], base[i] + down[i]]
    return out


def upsample_kernel(rel, before, own, after, interp, cosine, sine, out, weight, total):
    slots = before.shape[0] // 128

    @pl.when(pl.program_id(0) == 0)
    def _():
        weight[...] = jnp.zeros_like(weight)
        for j in range(16):
            for b in range(4):
                start = pl.multiple_of(rel[j * 4 + b] * 128, 128)
                weight[j // 4, pl.ds(start, 128), pl.ds((j % 4) * 128, 128)] = interp[j, b]

    row = lax.broadcasted_iota(jnp.int32, (8, 128), 0)
    low = row < 4
    for c in range(4):
        parts = []
        first, last = c, c + 5
        if first < 2:
            parts.append((before, first * 128, (2 - first) * 128, 0))
        lo, hi = max(first, 2), min(last, 6)
        parts.append((own, (lo - 2) * 128, (hi - lo) * 128, (lo - first) * 128))
        if last > 6:
            parts.append((after, 0, (last - 6) * 128, (6 - first) * 128))
        acc = None
        for ref, col, width, at in parts:
            piece = jnp.dot(
                ref[:, pl.ds(col, width)],
                weight[c, pl.ds(at, width), :],
                preferred_element_type=jnp.float32,
            )
            acc = piece if acc is None else acc + piece
        total[...] = acc

        def one(step, carry, c=c):
            pair = step // 4
            tile = step % 4
            lane = pl.multiple_of(tile * 128, 128)
            wide = pl.multiple_of(c * 512 + tile * 128, 128)
            halves = [[], []]
            for k in range(2):
                re = jnp.zeros((8, 128), jnp.float32)
                im = jnp.zeros((8, 128), jnp.float32)
                for h in range(8):
                    base = pl.multiple_of((pair * 2 + k) * 128 + h * 16, 16)
                    ur = total[pl.ds(base, 8), pl.ds(lane, 128)]
                    ui = total[pl.ds(base + 8, 8), pl.ds(lane, 128)]
                    cs = jnp.broadcast_to(cosine[h : h + 1, pl.ds(wide, 128)], (8, 128))
                    sn = jnp.broadcast_to(sine[h : h + 1, pl.ds(wide, 128)], (8, 128))
                    re = re + (cs * ur - sn * ui)
                    im = im + (sn * ur + cs * ui)
                halves[0].append(jnp.where(low, re, pltpu.roll(im, 4, 0)))
                halves[1].append(jnp.where(low, pltpu.roll(re, 4, 0), im))
            rows = pl.ds(pl.multiple_of(pair * 16, 16), 16)
            for k in range(2):
                value = jnp.concatenate(halves[k], axis=0).astype(jnp.bfloat16)
                out[(c * 4 + tile) * 2 + k, rows, :] = value
            return carry

        lax.fori_loop(0, (slots // 2) * 4, one, 0)


def upsample(before, own, after, interp, rel, cosine, sine):
    rows = own.shape[0]
    chunk = 512
    grid_spec = pltpu.PrefetchScalarGridSpec(
        num_scalar_prefetch=1,
        grid=(rows // chunk,),
        in_specs=[
            pl.BlockSpec((chunk, 256), lambda i, r: (i, 0)),
            pl.BlockSpec((chunk, 512), lambda i, r: (i, 0)),
            pl.BlockSpec((chunk, 256), lambda i, r: (i, 0)),
            pl.BlockSpec((16, 4, 128, 128), lambda i, r: (0, 0, 0, 0)),
            pl.BlockSpec((8, 2048), lambda i, r: (0, 0)),
            pl.BlockSpec((8, 2048), lambda i, r: (0, 0)),
        ],
        out_specs=pl.BlockSpec((32, chunk // 16, 128), lambda i, r: (0, i, 0)),
        scratch_shapes=[
            pltpu.VMEM((4, 640, 512), jnp.bfloat16),
            pltpu.VMEM((chunk, 512), jnp.float32),
        ],
    )
    return pl.pallas_call(
        upsample_kernel,
        grid_spec=grid_spec,
        out_shape=jax.ShapeDtypeStruct((32, rows // 16, 128), jnp.bfloat16),
    )(rel, before, own, after, interp, cosine, sine)


def translate_kernel(chunk_id, slot_parent, occupied, pats, table, out, grid_x, lines, spec, tab_z, tab):
    row = lax.broadcasted_iota(jnp.int32, (8, 128), 0)
    sign = jnp.where(row < 4, -1.0, 1.0).astype(jnp.float32)
    row7 = lax.broadcasted_iota(jnp.int32, (7, 128), 0)
    far_x = (row7 < 2) | (row7 > 4)

    def place(i, carry):
        both = pats[pl.ds(pl.multiple_of(i * 16, 16), 16), :].astype(jnp.float32)
        for k in range(2):
            p = slot_parent[2 * i + k]
            grid_x[p] = both[8 * k : 8 * k + 8] * occupied[p]
        return carry

    lax.fori_loop(0, 256, place, 0, unroll=4)

    for part in range(2):
        for y in range(7):
            vals = []
            for z in range(7):
                t = table[part, pl.ds(y * 7 + z, 7, stride=49), :]
                if 2 <= y <= 4 and 2 <= z <= 4:
                    t = jnp.where(far_x, t, 0.0)
                vals.append(t)
            for f, v in enumerate(line_kernel(vals)):
                tab_z[(part * 7 + y) * F1 + f, 0:7, :] = v

    def table_y(i, carry):
        part, fz = i // F1, i % F1
        vals = line_kernel([tab_z[(part * 7 + y) * F1 + fz] for y in range(7)])
        for fy, v in enumerate(vals):
            tab[part, fy * F1 + fz] = v
        return carry

    lax.fori_loop(0, 2 * F1, table_y, 0)

    def in_z(i, carry):
        for f, v in enumerate(line_in([grid_x[i * 8 + z] for z in range(8)])):
            lines[i * F1 + f] = v
        return carry

    lax.fori_loop(0, 64, in_z, 0)

    def in_y(i, carry):
        x, fz = i // F1, i % F1
        vals = line_in([lines[(x * 8 + y) * F1 + fz] for y in range(8)])
        for fy, v in enumerate(vals):
            spec[fy * F1 + fz, x] = v
        return carry

    lax.fori_loop(0, 8 * F1, in_y, 0)

    def product(f, carry):
        src = [spec[f, q] for q in range(8)]
        direct, cross = [None] * 8, [None] * 8
        for d in range(-3, 4):
            a = jnp.broadcast_to(tab[0, f, d + 3 : d + 4, :], (8, 128))
            b = jnp.broadcast_to(tab[1, f, d + 3 : d + 4, :], (8, 128))
            for p in range(8):
                q = p + d
                if q < 0 or q > 7 or abs(q // 2 - p // 2) > 1:
                    continue
                u, w = a * src[q], b * src[q]
                direct[p] = u if direct[p] is None else direct[p] + u
                cross[p] = w if cross[p] is None else cross[p] + w
        for p in range(8):
            spec[f, p] = direct[p] + sign * pltpu.roll(cross[p], 4, 0)
        return carry

    lax.fori_loop(0, NF, product, 0, unroll=2)

    def out_y(i, carry):
        x, fz = i // F1, i % F1
        vals = line_out([spec[fy * F1 + fz, x] for fy in range(F1)])
        for y, v in enumerate(vals):
            lines[(x * 8 + y) * F1 + fz] = v
        return carry

    lax.fori_loop(0, 8 * F1, out_y, 0)

    def out_z(i, carry):
        for z, v in enumerate(line_out([lines[i * F1 + f] for f in range(F1)])):
            grid_x[i * 8 + z] = v
        return carry

    lax.fori_loop(0, 64, out_z, 0)

    def give(i, carry):
        vals = [grid_x[slot_parent[2 * i + k]] for k in range(2)]
        both = jnp.concatenate(vals, axis=0).astype(out.dtype)
        out[pl.ds(pl.multiple_of(i * 16, 16), 16), :] = both
        return carry

    lax.fori_loop(0, 256, give, 0, unroll=4)


def translate(pats, table, chunk_id, slot_parent, occupied):
    grid_spec = pltpu.PrefetchScalarGridSpec(
        num_scalar_prefetch=3,
        grid=(1,),
        in_specs=[
            pl.BlockSpec((4096, 128), lambda i, c, s, o: (0, 0)),
            pl.BlockSpec((2, 343, 128), lambda i, c, s, o: (0, 0, c[0])),
        ],
        out_specs=pl.BlockSpec((4096, 128), lambda i, c, s, o: (0, 0)),
        scratch_shapes=[
            pltpu.VMEM((512, 8, 128), jnp.float32),
            pltpu.VMEM((64 * F1, 8, 128), jnp.float32),
            pltpu.VMEM((NF, 8, 8, 128), jnp.float32),
            pltpu.VMEM((14 * F1, 8, 128), jnp.float32),
            pltpu.VMEM((2, NF, 8, 128), jnp.float32),
        ],
    )
    return pl.pallas_call(
        translate_kernel,
        grid_spec=grid_spec,
        out_shape=jax.ShapeDtypeStruct((4096, 128), jnp.bfloat16),
    )(chunk_id, slot_parent, occupied, pats, table)


def arrange_kernel(got, out):
    low = lax.broadcasted_iota(jnp.int32, (8, 128), 0) < 4
    for pair in range(got.shape[1] // 16):
        for c in range(16):
            first = got[2 * c, pair * 16 : pair * 16 + 16, :].astype(jnp.float32)
            second = got[2 * c + 1, pair * 16 : pair * 16 + 16, :].astype(jnp.float32)
            for k in range(2):
                h0, h1 = first[8 * k : 8 * k + 8], second[8 * k : 8 * k + 8]
                s = pair * 2 + k
                out[s, 0, :, c * 128 : c * 128 + 128] = jnp.where(low, h0, pltpu.roll(h1, 4, 0))
                out[s, 1, :, c * 128 : c * 128 + 128] = jnp.where(low, pltpu.roll(h0, 4, 0), h1)


def arrange(got):
    return pl.pallas_call(
        arrange_kernel,
        grid=(4,),
        in_specs=[pl.BlockSpec((32, 32, 128), lambda i: (0, i, 0))],
        out_specs=pl.BlockSpec((4, 2, 8, 2048), lambda i: (i, 0, 0, 0)),
        out_shape=jax.ShapeDtypeStruct((16, 2, 8, 2048), jnp.float32),
    )(got)


def shards(child_pat, interp, interp_blocks, shift_angle, slot_parent, far_list, trans):
    dirs = lax.axis_size("dir")
    up = [(i, (i + 1) % dirs) for i in range(dirs)]
    down = [(j, i) for i, j in up]
    flat = child_pat.reshape(2048, 512)
    before = lax.ppermute(flat[:, 256:], "dir", up)
    after = lax.ppermute(flat[:, :256], "dir", down)
    centre = lax.axis_index("dir") * 4 + jnp.arange(16, dtype=jnp.int32)[:, None] // 4
    rel = ((interp_blocks - centre + 2) % 16).reshape(64)
    pieces = upsample(before, flat, after, interp, rel, jnp.cos(shift_angle), jnp.sin(shift_angle))
    pats = lax.all_to_all(pieces, "box", 0, 0, tiled=True).reshape(4096, 128)
    ident = jnp.arange(512, dtype=jnp.int32)[:, None]
    watch = jnp.concatenate([far_list[128:], far_list[256:384]], axis=0)
    occupied = jnp.any(watch == ident, axis=1).astype(jnp.float32)
    chunk_id = (lax.axis_index("box") // 2).astype(jnp.int32).reshape(1)
    local = translate(pats, trans, chunk_id, slot_parent, occupied)
    back = lax.all_to_all(local.reshape(32, 128, 128), "box", 0, 0, tiled=True)
    return arrange(back)


def solution(mesh):
    in_specs = (
        P("box", None, None, "dir"),
        P("dir", None, None, None),
        P("dir", None),
        P(None, "dir"),
        P(),
        P(),
        P(None, None, "dir"),
    )
    out_specs = P("box", None, None, "dir")
    return jax.shard_map(shards, mesh=mesh, in_specs=in_specs, out_specs=out_specs, check_vma=False)
```

```python
import jax
import jax.numpy as jnp
from jax import lax
from jax.experimental import pallas as pl
from jax.experimental.pallas import tpu as pltpu
from jax.sharding import PartitionSpec as P

G = 8
F1 = 18
NF = F1 * F1


def toom_in(v):
    a, b = v[0] + v[2], v[1] + v[3]
    c, d = v[0] + 4.0 * v[2], 2.0 * v[1] + 8.0 * v[3]
    return [v[0], v[3], a + b, a - b, c + d, c - d]


def line_in(x):
    even, odd = x[0::2], x[1::2]
    both = [e + o for e, o in zip(even, odd)]
    return toom_in(both) + toom_in(odd) + toom_in(even)


def toom_kernel(k):
    h2, h1, h0 = k
    a, b = (h0 + h2) * 0.5, h1 * 0.5
    c, d = (h0 + 4.0 * h2) * (1.0 / 24.0), h1 * (1.0 / 12.0)
    return [h0, h2, a + b, a - b, c + d, c - d]


def line_kernel(t):
    k0 = [t[1], t[3], t[5]]
    up = [t[2] - t[1], t[4] - t[3], t[6] - t[5]]
    down = [t[0] - t[1], t[2] - t[3], t[4] - t[5]]
    return toom_kernel(k0) + toom_kernel(up) + toom_kernel(down)


def toom_out(m):
    z0, z5 = m[0], m[1]
    e1, o1 = m[2] + m[3], m[2] - m[3]
    e2, d2 = m[4] + m[5], m[4] - m[5]
    z4 = e2 - e1 * (1.0 / 3.0) + z0 * 0.25
    z2 = e1 - z0 - z4
    z3 = 2.0 * d2 - o1 * (1.0 / 3.0) - 5.0 * z5
    z1 = o1 - z3 - z5
    return [z1, z2, z3, z4]


def line_out(m):
    base, up, down = toom_out(m[0:6]), toom_out(m[6:12]), toom_out(m[12:18])
    out = []
    for i in range(4):
        out += [base[i] + up[i], base[i] + down[i]]
    return out


CHUNKS = 4


def all_signal(bb, count):
    barrier = pltpu.get_barrier_semaphore()

    def one(k, carry):
        pl.semaphore_signal(barrier, 1, device_id={"box": (bb + k) % count})
        return carry

    lax.fori_loop(1, count, one, 0)
    return barrier


def gather_kernel(
    child, interp, sel, angle, trans, out, tab_out,
    own, before, after, weights, weight, total, stage, cosine, sine, raw, tab_z, tab,
    load_sem, halo_send, halo_recv, move_send, move_recv, local_sem,
):
    bb, dd = lax.axis_index("box"), lax.axis_index("dir")
    boxes, dirs = lax.axis_size("box"), lax.axis_size("dir")
    rows = 2048 // CHUNKS
    barrier = all_signal(bb, boxes)
    above, below = (dd + 1) % dirs, (dd + dirs - 1) % dirs
    pl.semaphore_signal(barrier, 1, device_id={"dir": above})
    pl.semaphore_signal(barrier, 1, device_id={"dir": below})
    first = pl.multiple_of((bb // 2) * 128, 128)
    loads = [
        pltpu.make_async_copy(trans.at[:, :, pl.ds(first, 128)], raw, load_sem.at[0]),
        pltpu.make_async_copy(interp, weights, load_sem.at[1]),
        pltpu.make_async_copy(child, own, load_sem.at[2]),
    ]
    for copy in loads:
        copy.start()
    pl.semaphore_wait(barrier, boxes + 1)

    def halo(i):
        at = pl.ds(pl.multiple_of(i * rows, rows), rows)
        return [
            pltpu.make_async_remote_copy(
                child.at[at, pl.ds(256, 256)], before.at[at, :],
                halo_send.at[0, i], halo_recv.at[0, i], device_id={"dir": above},
            ),
            pltpu.make_async_remote_copy(
                child.at[at, pl.ds(0, 256)], after.at[at, :],
                halo_send.at[1, i], halo_recv.at[1, i], device_id={"dir": below},
            ),
        ]

    for i in range(CHUNKS):
        for copy in halo(i):
            copy.start()

    cosine[...] = jnp.cos(angle[...])
    sine[...] = jnp.sin(angle[...])
    loads[0].wait()
    for x in range(2, 5):
        for y in range(2, 5):
            for z in range(2, 5):
                raw[x * 49 + y * 7 + z] = jnp.zeros((2, 128), jnp.float32)

    def table_x(i, carry):
        t = [raw[x * 49 + i] for x in range(7)]
        vals = [t[1], t[3], t[5], t[2] - t[1], t[4] - t[3], t[6] - t[5]]
        vals += [t[0] - t[1], t[2] - t[3], t[4] - t[5]]
        for g, v in enumerate(vals):
            tab[i, g] = v
        return carry

    lax.fori_loop(0, 49, table_x, 0)

    def table_z(y, carry):
        def inner(g, carry):
            vals = line_kernel([tab[y * 7 + z, g] for z in range(7)])
            for fz, v in enumerate(vals):
                tab_z[y * F1 + fz, g] = v
            return carry

        return lax.fori_loop(0, 9, inner, carry)

    lax.fori_loop(0, 7, table_z, 0)

    def table_y(fz, carry):
        def inner(g, carry):
            vals = line_kernel([tab_z[y * F1 + fz, g] for y in range(7)])
            for fy, v in enumerate(vals):
                tab[fy * F1 + fz, g] = v
            return carry

        return lax.fori_loop(0, 9, inner, carry)

    lax.fori_loop(0, F1, table_y, 0)
    loads[1].wait()
    for j in range(16):
        for o in range(5):
            value = None
            for b in (o - 1, o):
                if 0 <= b < 4:
                    term = weights[j, b].astype(jnp.float32) * sel[(j * 5 + o) * 2 + (b == o)]
                    value = term if value is None else value + term
            lanes = pl.ds((j % 4) * 128, 128)
            weight[j // 4, pl.ds(o * 128, 128), lanes] = value.astype(jnp.bfloat16)
    keep = pltpu.make_async_copy(tab, tab_out, load_sem.at[3])
    keep.start()
    loads[2].wait()
    low = lax.broadcasted_iota(jnp.int32, (8, 128), 0) < 4

    def chunk(i, carry):
        for copy in halo(i):
            copy.wait_recv()
        at = pl.ds(pl.multiple_of(i * rows, rows), rows)
        for c in range(4):
            parts = []
            if c < 2:
                parts.append((before, c * 128, (2 - c) * 128, 0))
            lo, hi = max(c, 2), min(c + 5, 6)
            parts.append((own, (lo - 2) * 128, (hi - lo) * 128, (lo - c) * 128))
            if c > 1:
                parts.append((after, 0, (c - 1) * 128, (6 - c) * 128))
            acc = None
            for ref, col, width, wrow in parts:
                piece = jnp.dot(
                    ref[at, pl.ds(col, width)],
                    weight[c, pl.ds(wrow, width), :],
                    preferred_element_type=jnp.float32,
                )
                acc = piece if acc is None else acc + piece
            total[...] = acc

            def tile_of(tile, carry, c=c):
                lane = pl.multiple_of(tile * 128, 128)
                wide = pl.multiple_of(c * 512 + tile * 128, 128)
                for pair in range(rows // 256):
                    halves = [[], []]
                    for k in range(2):
                        re = im = None
                        for h in range(8):
                            base = (pair * 2 + k) * 128 + h * 16
                            ur = total[pl.ds(base, 8), pl.ds(lane, 128)]
                            ui = total[pl.ds(base + 8, 8), pl.ds(lane, 128)]
                            cs = jnp.broadcast_to(cosine[h : h + 1, pl.ds(wide, 128)], (8, 128))
                            sn = jnp.broadcast_to(sine[h : h + 1, pl.ds(wide, 128)], (8, 128))
                            r, m = cs * ur - sn * ui, sn * ur + cs * ui
                            re = r if re is None else re + r
                            im = m if im is None else im + m
                        halves[0].append(jnp.where(low, re, pltpu.roll(im, 4, 0)))
                        halves[1].append(jnp.where(low, pltpu.roll(re, 4, 0), im))
                    where = pl.ds(pl.multiple_of(i * (rows // 16) + pair * 16, 16), 16)
                    for k in range(2):
                        value = jnp.concatenate(halves[k], axis=0).astype(jnp.bfloat16)
                        stage[(c * 4 + tile) * 2 + k, where, :] = value
                return carry

            lax.fori_loop(0, 4, tile_of, 0)

        piece = pl.ds(pl.multiple_of(i * (rows // 16), rows // 16), rows // 16)

        def send(k, carry):
            peer = (bb + k) % boxes
            pltpu.make_async_remote_copy(
                stage.at[peer, piece, :], out.at[bb, piece, :], move_send, move_recv,
                device_id={"box": peer},
            ).start()
            return carry

        lax.fori_loop(1, boxes, send, 0)
        return carry

    lax.fori_loop(0, CHUNKS, chunk, 0)
    mine = pltpu.make_async_copy(stage.at[bb], out.at[bb], local_sem)
    mine.start()
    mine.wait()
    keep.wait()
    for i in range(CHUNKS):
        for copy in halo(i):
            copy.wait_send()
    most = pl.ds(0, boxes - 1)
    pltpu.make_async_copy(stage.at[most], stage.at[most], move_send).wait()
    pltpu.make_async_copy(out.at[most], out.at[most], move_recv).wait()


def gather(child, interp, sel, angle, trans):
    any_space = pl.BlockSpec(memory_space=pl.ANY)
    return pl.pallas_call(
        gather_kernel,
        in_specs=[
            any_space,
            any_space,
            pl.BlockSpec(memory_space=pltpu.SMEM),
            pl.BlockSpec(memory_space=pltpu.VMEM),
            any_space,
        ],
        out_specs=[any_space, any_space],
        out_shape=[
            jax.ShapeDtypeStruct((32, 128, 128), jnp.bfloat16),
            jax.ShapeDtypeStruct((NF, 9, 2, 128), jnp.float32),
        ],
        scratch_shapes=[
            pltpu.VMEM((2048, 512), jnp.bfloat16),
            pltpu.VMEM((2048, 256), jnp.bfloat16),
            pltpu.VMEM((2048, 256), jnp.bfloat16),
            pltpu.VMEM((16, 4, 128, 128), jnp.bfloat16),
            pltpu.VMEM((4, 640, 512), jnp.bfloat16),
            pltpu.VMEM((2048 // CHUNKS, 512), jnp.float32),
            pltpu.VMEM((32, 128, 128), jnp.bfloat16),
            pltpu.VMEM((8, 2048), jnp.float32),
            pltpu.VMEM((8, 2048), jnp.float32),
            pltpu.VMEM((343, 2, 128), jnp.float32),
            pltpu.VMEM((7 * F1, 9, 2, 128), jnp.float32),
            pltpu.VMEM((NF, 9, 2, 128), jnp.float32),
            pltpu.SemaphoreType.DMA((4,)),
            pltpu.SemaphoreType.DMA((2, CHUNKS)),
            pltpu.SemaphoreType.DMA((2, CHUNKS)),
            pltpu.SemaphoreType.DMA,
            pltpu.SemaphoreType.DMA,
            pltpu.SemaphoreType.DMA,
        ],
        compiler_params=pltpu.CompilerParams(collective_id=0, has_side_effects=True),
    )(child, interp, sel, angle, trans)


def translate_kernel(slot_parent, occupied, pats, table, out, grid_x, lines, spec, tab, sem):
    fetch = pltpu.make_async_copy(table, tab, sem)
    fetch.start()
    row = lax.broadcasted_iota(jnp.int32, (8, 128), 0)
    sign = jnp.where(row < 4, -1.0, 1.0).astype(jnp.float32)

    def place(i, carry):
        both = pats[pl.ds(pl.multiple_of(i * 16, 16), 16), :].astype(jnp.float32)
        for k in range(2):
            p = slot_parent[2 * i + k]
            grid_x[p] = both[8 * k : 8 * k + 8] * occupied[p]
        return carry

    lax.fori_loop(0, 256, place, 0, unroll=8)

    def in_z(i, carry):
        for f, v in enumerate(line_in([grid_x[i * 8 + z] for z in range(8)])):
            lines[i * F1 + f] = v
        return carry

    lax.fori_loop(0, 64, in_z, 0, unroll=4)

    def in_y(x, carry):
        def inner(fz, carry):
            vals = line_in([lines[(x * 8 + y) * F1 + fz] for y in range(8)])
            for fy, v in enumerate(vals):
                spec[fy * F1 + fz, x] = v
            return carry

        return lax.fori_loop(0, F1, inner, carry, unroll=3)

    lax.fori_loop(0, 8, in_y, 0)
    fetch.wait()

    def product(f, carry):
        src = [spec[f, q] for q in range(8)]
        turn = [sign * pltpu.roll(v, 4, 0) for v in src]
        sets = [
            ([src[2 * j] + src[2 * j + 1] for j in range(4)], [turn[2 * j] + turn[2 * j + 1] for j in range(4)]),
            (src[1::2], turn[1::2]),
            (src[0::2], turn[0::2]),
        ]
        sums = []
        for g, (x, t) in enumerate(sets):
            acc = [None] * 4
            for j in range(-1, 2):
                k = g * 3 + j + 1
                a = jnp.broadcast_to(tab[f, k, 0:1, :], (8, 128))
                b = jnp.broadcast_to(tab[f, k, 1:2, :], (8, 128))
                for i in range(4):
                    if 0 <= i + j < 4:
                        v = a * x[i + j] + b * t[i + j]
                        acc[i] = v if acc[i] is None else acc[i] + v
            sums.append(acc)
        for i in range(4):
            spec[f, 2 * i] = sums[0][i] + sums[1][i]
            spec[f, 2 * i + 1] = sums[0][i] + sums[2][i]
        return carry

    lax.fori_loop(0, NF, product, 0, unroll=2)

    def out_y(x, carry):
        def inner(fz, carry):
            vals = line_out([spec[fy * F1 + fz, x] for fy in range(F1)])
            for y, v in enumerate(vals):
                lines[(x * 8 + y) * F1 + fz] = v
            return carry

        return lax.fori_loop(0, F1, inner, carry, unroll=2)

    lax.fori_loop(0, 8, out_y, 0)

    def out_z(i, carry):
        for z, v in enumerate(line_out([lines[i * F1 + f] for f in range(F1)])):
            grid_x[i * 8 + z] = v
        return carry

    lax.fori_loop(0, 64, out_z, 0, unroll=2)

    def give(i, carry):
        vals = [grid_x[slot_parent[2 * i + k]] for k in range(2)]
        both = jnp.concatenate(vals, axis=0).astype(out.dtype)
        out[pl.ds(pl.multiple_of(i * 16, 16), 16), :] = both
        return carry

    lax.fori_loop(0, 256, give, 0, unroll=8)


def translate(pats, table, slot_parent, occupied):
    grid_spec = pltpu.PrefetchScalarGridSpec(
        num_scalar_prefetch=2,
        grid=(1,),
        in_specs=[
            pl.BlockSpec((4096, 128), lambda i, s, o: (0, 0)),
            pl.BlockSpec(memory_space=pl.ANY),
        ],
        out_specs=pl.BlockSpec((4096, 128), lambda i, s, o: (0, 0)),
        scratch_shapes=[
            pltpu.VMEM((512, 8, 128), jnp.float32),
            pltpu.VMEM((64 * F1, 8, 128), jnp.float32),
            pltpu.VMEM((NF, 8, 8, 128), jnp.float32),
            pltpu.VMEM((NF, 9, 2, 128), jnp.float32),
            pltpu.SemaphoreType.DMA,
        ],
    )
    return pl.pallas_call(
        translate_kernel,
        grid_spec=grid_spec,
        out_shape=jax.ShapeDtypeStruct((4096, 128), jnp.bfloat16),
    )(slot_parent, occupied, pats, table)


def return_kernel(src, out, send_sem, recv_sem, local_sem):
    bb = lax.axis_index("box")
    boxes = lax.axis_size("box")
    barrier = all_signal(bb, boxes)
    mine = pltpu.make_async_copy(src.at[bb], out.at[bb], local_sem)
    mine.start()
    pl.semaphore_wait(barrier, boxes - 1)

    def send(k, carry):
        peer = (bb + k) % boxes
        pltpu.make_async_remote_copy(
            src.at[peer], out.at[bb], send_sem, recv_sem, device_id={"box": peer}
        ).start()
        return carry

    lax.fori_loop(1, boxes, send, 0)
    mine.wait()
    most = pl.ds(0, boxes - 1)
    pltpu.make_async_copy(src.at[most], src.at[most], send_sem).wait()
    pltpu.make_async_copy(out.at[most], out.at[most], recv_sem).wait()


def give_back(src):
    any_space = pl.BlockSpec(memory_space=pl.ANY)
    return pl.pallas_call(
        return_kernel,
        in_specs=[any_space],
        out_specs=any_space,
        out_shape=jax.ShapeDtypeStruct(src.shape, src.dtype),
        scratch_shapes=[pltpu.SemaphoreType.DMA] * 3,
        compiler_params=pltpu.CompilerParams(collective_id=1, has_side_effects=True),
    )(src)


def arrange_kernel(got, out):
    low = lax.broadcasted_iota(jnp.int32, (8, 128), 0) < 4
    for pair in range(got.shape[1] // 16):
        for c in range(16):
            first = got[2 * c, pair * 16 : pair * 16 + 16, :].astype(jnp.float32)
            second = got[2 * c + 1, pair * 16 : pair * 16 + 16, :].astype(jnp.float32)
            for k in range(2):
                h0, h1 = first[8 * k : 8 * k + 8], second[8 * k : 8 * k + 8]
                s = pair * 2 + k
                out[s, 0, :, c * 128 : c * 128 + 128] = jnp.where(low, h0, pltpu.roll(h1, 4, 0))
                out[s, 1, :, c * 128 : c * 128 + 128] = jnp.where(low, pltpu.roll(h0, 4, 0), h1)


def arrange(got):
    return pl.pallas_call(
        arrange_kernel,
        grid=(4,),
        in_specs=[pl.BlockSpec((32, 32, 128), lambda i: (0, i, 0))],
        out_specs=pl.BlockSpec((4, 2, 8, 2048), lambda i: (i, 0, 0, 0)),
        out_shape=jax.ShapeDtypeStruct((16, 2, 8, 2048), jnp.float32),
    )(got)


def shards(child_pat, interp, interp_blocks, shift_angle, slot_parent, far_list, trans):
    centre = lax.axis_index("dir") * 4 + jnp.arange(16, dtype=jnp.int32)[:, None] // 4
    rel = (interp_blocks - centre + 2) % 16
    slots = jnp.arange(5, dtype=jnp.int32)[None, :, None]
    entry = jnp.clip(slots - 1 + jnp.arange(2, dtype=jnp.int32)[None, None, :], 0, 3)
    hit = jnp.sum((rel[:, None, None, :] == slots[..., None]) & (entry[..., None] == jnp.arange(4)), axis=3)
    sel = hit.astype(jnp.float32).reshape(160)
    pieces, table = gather(
        child_pat.reshape(2048, 512), interp, sel, shift_angle, jnp.transpose(trans, (1, 0, 2))
    )
    ident = jnp.arange(512, dtype=jnp.int32)[:, None]
    watch = jnp.concatenate([far_list[128:], far_list[256:384]], axis=0)
    occupied = jnp.any(watch == ident, axis=1).astype(jnp.float32)
    local = translate(pieces.reshape(4096, 128), table, slot_parent, occupied)
    return arrange(give_back(local.reshape(32, 128, 128)))


def solution(mesh):
    in_specs = (
        P("box", None, None, "dir"),
        P("dir", None, None, None),
        P("dir", None),
        P(None, "dir"),
        P(),
        P(),
        P(None, None, "dir"),
    )
    out_specs = P("box", None, None, "dir")
    return jax.shard_map(shards, mesh=mesh, in_specs=in_specs, out_specs=out_specs, check_vma=False)
```

```python
import jax
import jax.numpy as jnp
from jax import lax
from jax.experimental import pallas as pl
from jax.experimental.pallas import tpu as pltpu
from jax.sharding import PartitionSpec as P

G = 8
F1 = 18
NF = F1 * F1


def toom_in(v):
    a, b = v[0] + v[2], v[1] + v[3]
    c, d = v[0] + 4.0 * v[2], 2.0 * v[1] + 8.0 * v[3]
    return [v[0], v[3], a + b, a - b, c + d, c - d]


def line_in(x):
    even, odd = x[0::2], x[1::2]
    both = [e + o for e, o in zip(even, odd)]
    return toom_in(both) + toom_in(odd) + toom_in(even)


def toom_kernel(k):
    h2, h1, h0 = k
    a, b = (h0 + h2) * 0.5, h1 * 0.5
    c, d = (h0 + 4.0 * h2) * (1.0 / 24.0), h1 * (1.0 / 12.0)
    return [h0, h2, a + b, a - b, c + d, c - d]


def line_kernel(t):
    k0 = [t[1], t[3], t[5]]
    up = [t[2] - t[1], t[4] - t[3], t[6] - t[5]]
    down = [t[0] - t[1], t[2] - t[3], t[4] - t[5]]
    return toom_kernel(k0) + toom_kernel(up) + toom_kernel(down)


def toom_out(m):
    z0, z5 = m[0], m[1]
    e1, o1 = m[2] + m[3], m[2] - m[3]
    e2, d2 = m[4] + m[5], m[4] - m[5]
    z4 = e2 - e1 * (1.0 / 3.0) + z0 * 0.25
    z2 = e1 - z0 - z4
    z3 = 2.0 * d2 - o1 * (1.0 / 3.0) - 5.0 * z5
    z1 = o1 - z3 - z5
    return [z1, z2, z3, z4]


def line_out(m):
    base, up, down = toom_out(m[0:6]), toom_out(m[6:12]), toom_out(m[12:18])
    out = []
    for i in range(4):
        out += [base[i] + up[i], base[i] + down[i]]
    return out


TURNS = [(1, 1), (3, 1), (3, 3), (1, 3), (2, 2), (1, 2), (2, 1), (3, 2), (2, 3), (1, 0), (0, 1), (3, 0), (0, 3), (2, 0), (0, 2)]
PEERS = [(0, 0, 1)] + [(x, z, c) for c in range(2) for x, z in TURNS]
CHUNKS = 8


def peers_of(bb):
    x, z, c = bb // 8, (bb // 2) % 4, bb % 2
    return [((x + dx) % 4) * 8 + ((z + dz) % 4) * 2 + (c + dc) % 2 for dx, dz, dc in PEERS]


def main_kernel(
    child, interp, blocks_in, angle_in, slot_in, far, trans, out,
    own, before, after, weights, weight, total, stage, cosine, sine, raw, tab_z, tab, tiles,
    listed, occ, mask, slot_vec, slot_of, blocks, angle, slot_parent,
    pats, wide_x, later, grid_x, lines, spec, back,
    load_sem, halo_send, halo_recv, move_send, move_recv, local_sem, home_sem, back_send, back_recv,
):
    bb, dd = lax.axis_index("box"), lax.axis_index("dir")
    dirs = lax.axis_size("dir")
    rows = 2048 // CHUNKS
    peers = peers_of(bb)
    above, below = (dd + 1) % dirs, (dd + dirs - 1) % dirs
    barrier = pltpu.get_barrier_semaphore()
    pl.semaphore_signal(barrier, 1, device_id={"dir": above})
    pl.semaphore_signal(barrier, 1, device_id={"dir": below})
    for peer in peers:
        pl.semaphore_signal(barrier, 1, device_id={"box": peer})
    first = pl.multiple_of((bb // 2) * 128, 128)
    loads = [
        pltpu.make_async_copy(trans.at[:, :, pl.ds(first, 128)], raw, load_sem.at[0]),
        pltpu.make_async_copy(interp, weights, load_sem.at[1]),
        pltpu.make_async_copy(child, own, load_sem.at[2]),
        pltpu.make_async_copy(far, listed, load_sem.at[3]),
        pltpu.make_async_copy(blocks_in, blocks, load_sem.at[4]),
        pltpu.make_async_copy(slot_in, slot_parent, load_sem.at[5]),
        pltpu.make_async_copy(angle_in, angle, load_sem.at[6]),
    ]
    for copy in loads:
        copy.start()
    pl.semaphore_wait(barrier, len(peers) + 2)

    def halo(i):
        at = pl.ds(pl.multiple_of(i * rows, rows), rows)
        return [
            pltpu.make_async_remote_copy(
                child.at[at, pl.ds(256, 256)], before.at[at, :],
                halo_send.at[0, i], halo_recv.at[0, i], device_id={"dir": above},
            ),
            pltpu.make_async_remote_copy(
                child.at[at, pl.ds(0, 256)], after.at[at, :],
                halo_send.at[1, i], halo_recv.at[1, i], device_id={"dir": below},
            ),
        ]

    for i in range(CHUNKS):
        for copy in halo(i):
            copy.start()

    loads[6].wait()
    cosine[...] = jnp.cos(angle[...])
    sine[...] = jnp.sin(angle[...])
    loads[1].wait()
    loads[4].wait()
    for j in range(16):
        rel = [(blocks[b, j] - (dd * 4 + j // 4) + 18) & 15 for b in range(4)]
        for o in range(5):
            value = None
            for b in (o - 1, o):
                if 0 <= b < 4:
                    term = weights[j, b].astype(jnp.float32) * jnp.where(rel[b] == o, 1.0, 0.0)
                    value = term if value is None else value + term
            lanes = pl.ds((j % 4) * 128, 128)
            weight[j // 4, pl.ds(o * 128, 128), lanes] = value.astype(jnp.bfloat16)

    loads[3].wait()
    loads[5].wait()
    lane = lax.broadcasted_iota(jnp.int32, (189, 128), 1)
    for t in range(4):
        watch = listed[:, pl.ds((t + 1 if t < 3 else 2) * 128, 128)]
        occ[t : t + 1, :] = jnp.max(jnp.where(watch == lane + t * 128, 1.0, 0.0), axis=0, keepdims=True)
    ident = lax.broadcasted_iota(jnp.int32, (4, 128), 0) * 128 + lax.broadcasted_iota(jnp.int32, (4, 128), 1)
    for s in range(16):
        held = jnp.where(ident == slot_parent[bb * 16 + s], occ[...], 0.0)
        held = jnp.max(jnp.max(held, axis=1, keepdims=True), axis=0, keepdims=True)
        mask[s] = jnp.broadcast_to(held, (8, 128))

    def invert(i, found):
        return tuple(
            jnp.where(ident == slot_parent[i * 4 + k], i * 4 + k, found[k]) for k in range(4)
        )

    zero = jnp.zeros((4, 128), jnp.int32)
    found = lax.fori_loop(0, 128, invert, (zero,) * 4, unroll=4)
    slot_vec[...] = jnp.maximum(jnp.maximum(found[0], found[1]), jnp.maximum(found[2], found[3]))
    to_scalar = [
        pltpu.make_async_copy(slot_vec.at[t], slot_of.at[pl.ds(t * 128, 128)], load_sem.at[7 + t])
        for t in range(4)
    ]
    for copy in to_scalar:
        copy.start()

    loads[0].wait()
    for x in range(2, 5):
        for y in range(2, 5):
            for z in range(2, 5):
                raw[x * 49 + y * 7 + z] = jnp.zeros((2, 128), jnp.float32)

    def table_x(i, carry):
        t = [raw[x * 49 + i] for x in range(7)]
        vals = [t[1], t[3], t[5], t[2] - t[1], t[4] - t[3], t[6] - t[5]]
        vals += [t[0] - t[1], t[2] - t[3], t[4] - t[5]]
        for g, v in enumerate(vals):
            tab[i, g] = v
        return carry

    lax.fori_loop(0, 49, table_x, 0)

    def table_z(y, carry):
        def inner(g, carry):
            vals = line_kernel([tab[y * 7 + z, g] for z in range(7)])
            for fz, v in enumerate(vals):
                tab_z[y * F1 + fz, g] = v
            return carry

        return lax.fori_loop(0, 9, inner, carry, unroll=3)

    lax.fori_loop(0, 7, table_z, 0)

    def table_y(fz, carry):
        def inner(g, carry):
            vals = line_kernel([tab_z[y * F1 + fz, g] for y in range(7)])
            for fy, v in enumerate(vals):
                tab[fy * F1 + fz, g] = v
            return carry

        return lax.fori_loop(0, 9, inner, carry, unroll=3)

    lax.fori_loop(0, F1, table_y, 0)
    loads[2].wait()
    row = lax.broadcasted_iota(jnp.int32, (8, 128), 0)
    low = row < 4

    def chunk(i, carry):
        for copy in halo(i):
            copy.wait_recv()
        at = pl.ds(pl.multiple_of(i * rows, rows), rows)
        for c in range(4):
            parts = []
            if c < 2:
                parts.append((before, c * 128, (2 - c) * 128, 0))
            lo, hi = max(c, 2), min(c + 5, 6)
            parts.append((own, (lo - 2) * 128, (hi - lo) * 128, (lo - c) * 128))
            if c > 1:
                parts.append((after, 0, (c - 1) * 128, (6 - c) * 128))
            acc = None
            for ref, col, width, wrow in parts:
                piece = jnp.dot(
                    ref[at, pl.ds(col, width)],
                    weight[c, pl.ds(wrow, width), :],
                    preferred_element_type=jnp.float32,
                )
                acc = piece if acc is None else acc + piece
            total[...] = acc

            def tile_of(tile, carry, c=c):
                lane = pl.multiple_of(tile * 128, 128)
                wide = pl.multiple_of(c * 512 + tile * 128, 128)
                halves = [[], []]
                for k in range(2):
                    re = im = None
                    for h in range(8):
                        base = k * 128 + h * 16
                        ur = total[pl.ds(base, 8), pl.ds(lane, 128)]
                        ui = total[pl.ds(base + 8, 8), pl.ds(lane, 128)]
                        cs = jnp.broadcast_to(cosine[h : h + 1, pl.ds(wide, 128)], (8, 128))
                        sn = jnp.broadcast_to(sine[h : h + 1, pl.ds(wide, 128)], (8, 128))
                        r, m = cs * ur - sn * ui, sn * ur + cs * ui
                        re = r if re is None else re + r
                        im = m if im is None else im + m
                    keep = mask[2 * i + k]
                    re, im = re * keep, im * keep
                    halves[0].append(jnp.where(low, re, pltpu.roll(im, 4, 0)))
                    halves[1].append(jnp.where(low, pltpu.roll(re, 4, 0), im))
                for k in range(2):
                    value = jnp.concatenate(halves[k], axis=0).astype(jnp.bfloat16)
                    stage[(c * 4 + tile) * 2 + k, i] = value
                return carry

            lax.fori_loop(0, 4, tile_of, 0)
        for peer in peers:
            pltpu.make_async_remote_copy(
                stage.at[peer, i], pats.at[bb * 8 + i], move_send, move_recv,
                device_id={"box": peer},
            ).start()
        return carry

    lax.fori_loop(0, CHUNKS, chunk, 0)
    mine = pltpu.make_async_copy(stage.at[bb], pats.at[pl.ds(bb * 8, 8)], local_sem)
    mine.start()
    pick = (row & 2) == 0

    def expand(fy, carry):
        def inner(fz, carry):
            for g in range(9):
                here, there = tab.at[fy * F1 + fz, g], tab.at[fy * F1 + fz + 9, g]
                two = []
                for part in range(2):
                    left = jnp.broadcast_to(here[part : part + 1, :], (8, 128))
                    right = jnp.broadcast_to(there[part : part + 1, :], (8, 128))
                    two.append(jnp.where(pick, left, right))
                tiles[fy * 9 + fz, g, 0] = two[0]
                tiles[fy * 9 + fz, g, 1] = jnp.where(low, -two[1], two[1])
            return carry

        return lax.fori_loop(0, 9, inner, carry)

    lax.fori_loop(0, F1, expand, 0)
    for copy in to_scalar:
        copy.wait()
    mine.wait()
    pltpu.make_async_copy(pats.at[pl.ds(0, 248)], pats.at[pl.ds(0, 248)], move_recv).wait()

    def widen(i, carry):
        both = pats[i].astype(jnp.float32)
        wide_x[2 * i] = both[0:8]
        wide_x[2 * i + 1] = both[8:16]
        return carry

    lax.fori_loop(0, 256, widen, 0, unroll=8)

    for half in range(2):

        def in_z(i, carry):
            vals = []
            for z in range(8):
                at = i * 8 + z
                if half == 0:
                    left, right = wide_x[slot_of[at]], wide_x[slot_of[at + 256]]
                    vals.append(jnp.where(pick, left, pltpu.roll(right, 2, 0)))
                    later[at] = jnp.where(pick, pltpu.roll(left, 6, 0), right)
                else:
                    vals.append(later[at])
            for f, v in enumerate(line_in(vals)):
                lines[i * F1 + f] = v
            return carry

        lax.fori_loop(0, 32, in_z, 0, unroll=4)

        def in_y(x, carry):
            def inner(fz, carry):
                vals = line_in([lines[(x * 8 + y) * F1 + fz] for y in range(8)])
                for fy, v in enumerate(vals):
                    spec[fy * F1 + fz, x] = v
                return carry

            return lax.fori_loop(0, F1, inner, carry, unroll=3)

        lax.fori_loop(0, 4, in_y, 0)

        def product(fy, carry):
            def inner(fz, carry):
                here, there = fy * F1 + fz, fy * F1 + fz + 9
                src = [None] * 8
                for x in range(4):
                    left, right = spec[here, x], spec[there, x]
                    src[x] = jnp.where(pick, left, pltpu.roll(right, 2, 0))
                    src[x + 4] = jnp.where(pick, pltpu.roll(left, 6, 0), right)
                turn = [pltpu.roll(v, 4, 0) for v in src]
                sets = [
                    ([src[2 * j] + src[2 * j + 1] for j in range(4)], [turn[2 * j] + turn[2 * j + 1] for j in range(4)]),
                    (src[1::2], turn[1::2]),
                    (src[0::2], turn[0::2]),
                ]
                sums = []
                for g, (x, t) in enumerate(sets):
                    acc = [None] * 4
                    for j in range(-1, 2):
                        a = tiles[fy * 9 + fz, g * 3 + j + 1, 0]
                        b = tiles[fy * 9 + fz, g * 3 + j + 1, 1]
                        for i in range(4):
                            if 0 <= i + j < 4:
                                v = a * x[i + j] + b * t[i + j]
                                acc[i] = v if acc[i] is None else acc[i] + v
                    sums.append(acc)
                res = []
                for i in range(4):
                    res += [sums[0][i] + sums[1][i], sums[0][i] + sums[2][i]]
                for x in range(4):
                    spec[here, x] = jnp.where(pick, res[x], pltpu.roll(res[x + 4], 2, 0))
                    spec[there, x] = jnp.where(pick, pltpu.roll(res[x], 6, 0), res[x + 4])
                return carry

            return lax.fori_loop(0, 9, inner, carry, unroll=9)

        lax.fori_loop(0, F1, product, 0)

        def out_y(x, carry):
            def inner(fz, carry):
                vals = line_out([spec[fy * F1 + fz, x] for fy in range(F1)])
                for y, v in enumerate(vals):
                    lines[(x * 8 + y) * F1 + fz] = v
                return carry

            return lax.fori_loop(0, F1, inner, carry, unroll=3)

        lax.fori_loop(0, 4, out_y, 0)

        def out_z(i, carry):
            for z, v in enumerate(line_out([lines[i * F1 + f] for f in range(F1)])):
                grid_x[i * 8 + z] = v
                grid_x[256 + i * 8 + z] = pltpu.roll(v, 6, 0)
            return carry

        lax.fori_loop(0, 32, out_z, 0, unroll=4)

        def give(target, half=half):
            for q in range(4):
                vals = [grid_x[slot_parent[target * 16 + 4 * q + k]] for k in range(4)]
                pairs = [jnp.where(pick, vals[k], pltpu.roll(vals[k + 1], 2, 0)) for k in (0, 2)]
                back[half, target, q] = jnp.concatenate(pairs, axis=0).astype(jnp.bfloat16)

        for peer in peers:
            give(peer)
            pltpu.make_async_remote_copy(
                back.at[half, peer], out.at[half, bb], back_send.at[half], back_recv.at[half],
                device_id={"box": peer},
            ).start()
        give(bb)
        pltpu.make_async_copy(back.at[half, bb], out.at[half, bb], home_sem.at[half]).start()

    for i in range(CHUNKS):
        for copy in halo(i):
            copy.wait_send()
    most = pl.ds(0, 31)
    pltpu.make_async_copy(stage.at[most], stage.at[most], move_send).wait()
    for half in range(2):
        pltpu.make_async_copy(back.at[half, bb], out.at[half, bb], home_sem.at[half]).wait()
        sent, got = back.at[half, most], out.at[half, most]
        pltpu.make_async_copy(sent, sent, back_send.at[half]).wait()
        pltpu.make_async_copy(got, got, back_recv.at[half]).wait()


def far_pieces(child, interp, blocks, angle, slot_parent, far, trans):
    any_space = pl.BlockSpec(memory_space=pl.ANY)
    return pl.pallas_call(
        main_kernel,
        in_specs=[any_space] * 7,
        out_specs=any_space,
        out_shape=jax.ShapeDtypeStruct((2, 32, 4, 16, 128), jnp.bfloat16),
        scratch_shapes=[
            pltpu.VMEM((2048, 512), jnp.bfloat16),
            pltpu.VMEM((2048, 256), jnp.bfloat16),
            pltpu.VMEM((2048, 256), jnp.bfloat16),
            pltpu.VMEM((16, 4, 128, 128), jnp.bfloat16),
            pltpu.VMEM((4, 640, 512), jnp.bfloat16),
            pltpu.VMEM((2048 // CHUNKS, 512), jnp.float32),
            pltpu.VMEM((32, 8, 16, 128), jnp.bfloat16),
            pltpu.VMEM((8, 2048), jnp.float32),
            pltpu.VMEM((8, 2048), jnp.float32),
            pltpu.VMEM((343, 2, 128), jnp.float32),
            pltpu.VMEM((7 * F1, 9, 2, 128), jnp.float32),
            pltpu.VMEM((NF, 9, 2, 128), jnp.float32),
            pltpu.VMEM((NF // 2, 9, 2, 8, 128), jnp.float32),
            pltpu.VMEM((189, 512), jnp.int32),
            pltpu.VMEM((4, 128), jnp.float32),
            pltpu.VMEM((16, 8, 128), jnp.float32),
            pltpu.VMEM((4, 128), jnp.int32),
            pltpu.SMEM((512,), jnp.int32),
            pltpu.SMEM((4, 16), jnp.int32),
            pltpu.VMEM((8, 2048), jnp.float32),
            pltpu.SMEM((512,), jnp.int32),
            pltpu.VMEM((256, 16, 128), jnp.bfloat16),
            pltpu.VMEM((512, 8, 128), jnp.float32),
            pltpu.VMEM((256, 8, 128), jnp.float32),
            pltpu.VMEM((512, 8, 128), jnp.float32),
            pltpu.VMEM((32 * F1, 8, 128), jnp.float32),
            pltpu.VMEM((NF, 4, 8, 128), jnp.float32),
            pltpu.VMEM((2, 32, 4, 16, 128), jnp.bfloat16),
            pltpu.SemaphoreType.DMA((11,)),
            pltpu.SemaphoreType.DMA((2, CHUNKS)),
            pltpu.SemaphoreType.DMA((2, CHUNKS)),
            pltpu.SemaphoreType.DMA,
            pltpu.SemaphoreType.DMA,
            pltpu.SemaphoreType.DMA,
            pltpu.SemaphoreType.DMA((2,)),
            pltpu.SemaphoreType.DMA((2,)),
            pltpu.SemaphoreType.DMA((2,)),
        ],
        compiler_params=pltpu.CompilerParams(collective_id=0, has_side_effects=True, vmem_limit_bytes=46 * 2**20),
    )(*[pltpu.with_memory_space_constraint(v, pltpu.HBM) for v in (child, interp, blocks, angle, slot_parent, far, trans)])


def arrange_kernel(src, dst, got, out, in_sem, out_sem):
    row = lax.broadcasted_iota(jnp.int32, (8, 128), 0)
    low, pick = row < 4, (row & 2) == 0

    def swap(a, b, mask, shift):
        return (
            jnp.where(mask, a, pltpu.roll(b, shift, 0)),
            jnp.where(mask, pltpu.roll(a, 8 - shift, 0), b),
        )

    fetch = [pltpu.make_async_copy(src.at[:, :, n], got.at[n], in_sem.at[n]) for n in range(4)]
    store = [pltpu.make_async_copy(out.at[pl.ds(4 * n, 4)], dst.at[pl.ds(4 * n, 4)], out_sem.at[n]) for n in range(4)]
    for copy in fetch:
        copy.start()
    for n in range(4):
        fetch[n].wait()
        for c in range(16):
            parts = [got[n, half, 2 * c + odd].astype(jnp.float32) for odd in range(2) for half in range(2)]
            lanes = slice(c * 128, c * 128 + 128)
            for k in range(2):
                v0, v1, v2, v3 = [v[8 * k : 8 * k + 8] for v in parts]
                p, r = swap(v0, v2, low, 4)
                q, s = swap(v1, v3, low, 4)
                at = 4 * n + 2 * k
                out[at, 0, :, lanes], out[at + 1, 0, :, lanes] = swap(p, q, pick, 2)
                out[at, 1, :, lanes], out[at + 1, 1, :, lanes] = swap(r, s, pick, 2)
        store[n].start()
    for copy in store:
        copy.wait()


def arrange(got):
    return pl.pallas_call(
        arrange_kernel,
        in_specs=[pl.BlockSpec(memory_space=pl.ANY)],
        out_specs=pl.BlockSpec(memory_space=pl.ANY),
        out_shape=jax.ShapeDtypeStruct((16, 2, 8, 2048), jnp.float32),
        scratch_shapes=[
            pltpu.VMEM((4, 2, 32, 16, 128), jnp.bfloat16),
            pltpu.VMEM((16, 2, 8, 2048), jnp.float32),
            pltpu.SemaphoreType.DMA((4,)),
            pltpu.SemaphoreType.DMA((4,)),
        ],
        compiler_params=pltpu.CompilerParams(vmem_limit_bytes=8 * 2**20),
    )(got)


def shards(child_pat, interp, interp_blocks, shift_angle, slot_parent, far_list, trans):
    pieces = far_pieces(
        child_pat.reshape(2048, 512),
        interp,
        interp_blocks.T,
        shift_angle,
        slot_parent,
        far_list.T,
        jnp.transpose(trans, (1, 0, 2)),
    )
    return arrange(pieces)


def solution(mesh):
    in_specs = (
        P("box", None, None, "dir"),
        P("dir", None, None, None),
        P("dir", None),
        P(None, "dir"),
        P(),
        P(),
        P(None, None, "dir"),
    )
    out_specs = P("box", None, None, "dir")
    return jax.shard_map(shards, mesh=mesh, in_specs=in_specs, out_specs=out_specs, check_vma=False)
```

```python
import jax
import jax.numpy as jnp
from jax import lax
from jax.experimental import pallas as pl
from jax.experimental.pallas import tpu as pltpu
from jax.sharding import PartitionSpec as P

G = 8
F1 = 18
NF = F1 * F1


def toom_in(v):
    a, b = v[0] + v[2], v[1] + v[3]
    c, d = v[0] + 4.0 * v[2], 2.0 * v[1] + 8.0 * v[3]
    return [v[0], v[3], a + b, a - b, c + d, c - d]


def line_in(x):
    even, odd = x[0::2], x[1::2]
    both = [e + o for e, o in zip(even, odd)]
    return toom_in(both) + toom_in(odd) + toom_in(even)


def toom_kernel(k):
    h2, h1, h0 = k
    a, b = (h0 + h2) * 0.5, h1 * 0.5
    c, d = (h0 + 4.0 * h2) * (1.0 / 24.0), h1 * (1.0 / 12.0)
    return [h0, h2, a + b, a - b, c + d, c - d]


def line_kernel(t):
    k0 = [t[1], t[3], t[5]]
    up = [t[2] - t[1], t[4] - t[3], t[6] - t[5]]
    down = [t[0] - t[1], t[2] - t[3], t[4] - t[5]]
    return toom_kernel(k0) + toom_kernel(up) + toom_kernel(down)


def toom_out(m):
    z0, z5 = m[0], m[1]
    e1, o1 = m[2] + m[3], m[2] - m[3]
    e2, d2 = m[4] + m[5], m[4] - m[5]
    z4 = e2 - e1 * (1.0 / 3.0) + z0 * 0.25
    z2 = e1 - z0 - z4
    z3 = 2.0 * d2 - o1 * (1.0 / 3.0) - 5.0 * z5
    z1 = o1 - z3 - z5
    return [z1, z2, z3, z4]


def line_out(m):
    base, up, down = toom_out(m[0:6]), toom_out(m[6:12]), toom_out(m[12:18])
    out = []
    for i in range(4):
        out += [base[i] + up[i], base[i] + down[i]]
    return out


TURNS = [(1, 1), (3, 1), (3, 3), (1, 3), (2, 2), (1, 2), (2, 1), (3, 2), (2, 3), (1, 0), (0, 1), (3, 0), (0, 3), (2, 0), (0, 2)]
PEERS = [(0, 0, 1)] + [(x, z, c) for c in range(2) for x, z in TURNS]
CHUNKS = 8


def peers_of(bb):
    x, z, c = bb // 8, (bb // 2) % 4, bb % 2
    return [((x + dx) % 4) * 8 + ((z + dz) % 4) * 2 + (c + dc) % 2 for dx, dz, dc in PEERS]


def main_kernel(
    child, interp, blocks_in, angle_in, slot_in, far, trans, out,
    own, before, after, weights, weight, total, stage, cosine, sine, raw, tab_z, tab, tiles,
    listed, occ, mask, slot_vec, slot_of, slot_parent, blocks, angle,
    pats, wide_x, later, grid_x, lines, spec, back,
    load_sem, halo_send, halo_recv, move_send, move_recv, local_sem, home_sem, back_send, back_recv,
):
    bb, dd = lax.axis_index("box"), lax.axis_index("dir")
    dirs = lax.axis_size("dir")
    rows = 2048 // CHUNKS
    peers = peers_of(bb)
    above, below = (dd + 1) % dirs, (dd + dirs - 1) % dirs
    barrier = pltpu.get_barrier_semaphore()
    pl.semaphore_signal(barrier, 1, device_id={"dir": above})
    pl.semaphore_signal(barrier, 1, device_id={"dir": below})
    for peer in peers:
        pl.semaphore_signal(barrier, 1, device_id={"box": peer})
    first = pl.multiple_of((bb // 2) * 128, 128)
    loads = [
        pltpu.make_async_copy(trans.at[:, :, pl.ds(first, 128)], raw, load_sem.at[0]),
        pltpu.make_async_copy(interp, weights, load_sem.at[1]),
        pltpu.make_async_copy(child, own, load_sem.at[2]),
        pltpu.make_async_copy(far, listed, load_sem.at[3]),
        pltpu.make_async_copy(blocks_in, blocks, load_sem.at[4]),
        pltpu.make_async_copy(slot_in, slot_parent, load_sem.at[5]),
        pltpu.make_async_copy(angle_in, angle, load_sem.at[6]),
    ]
    for copy in loads:
        copy.start()
    pl.semaphore_wait(barrier, len(peers) + 2)

    def halo(i):
        at = pl.ds(pl.multiple_of(i * rows, rows), rows)
        return [
            pltpu.make_async_remote_copy(
                child.at[at, pl.ds(256, 256)], before.at[at, :],
                halo_send.at[0, i], halo_recv.at[0, i], device_id={"dir": above},
            ),
            pltpu.make_async_remote_copy(
                child.at[at, pl.ds(0, 256)], after.at[at, :],
                halo_send.at[1, i], halo_recv.at[1, i], device_id={"dir": below},
            ),
        ]

    for i in range(CHUNKS):
        for copy in halo(i):
            copy.start()

    loads[6].wait()
    cosine[...] = jnp.cos(angle[...])
    sine[...] = jnp.sin(angle[...])
    loads[1].wait()
    loads[4].wait()
    for j in range(16):
        rel = [(blocks[b, j] - (dd * 4 + j // 4) + 18) & 15 for b in range(4)]
        for o in range(5):
            value = None
            for b in (o - 1, o):
                if 0 <= b < 4:
                    term = weights[j, b].astype(jnp.float32) * jnp.where(rel[b] == o, 1.0, 0.0)
                    value = term if value is None else value + term
            lanes = pl.ds((j % 4) * 128, 128)
            weight[j // 4, pl.ds(o * 128, 128), lanes] = value.astype(jnp.bfloat16)

    loads[3].wait()
    loads[5].wait()
    lane = lax.broadcasted_iota(jnp.int32, (189, 128), 1)
    for t in range(4):
        watch = listed[:, pl.ds((t + 1 if t < 3 else 2) * 128, 128)]
        occ[t : t + 1, :] = jnp.max(jnp.where(watch == lane + t * 128, 1.0, 0.0), axis=0, keepdims=True)
    ident = lax.broadcasted_iota(jnp.int32, (4, 128), 0) * 128 + lax.broadcasted_iota(jnp.int32, (4, 128), 1)
    for s in range(16):
        held = jnp.where(ident == slot_parent[bb * 16 + s], occ[...], 0.0)
        held = jnp.max(jnp.max(held, axis=1, keepdims=True), axis=0, keepdims=True)
        mask[s] = jnp.broadcast_to(held, (8, 128))

    def invert(i, found):
        return tuple(
            jnp.where(ident == slot_parent[i * 4 + k], i * 4 + k, found[k]) for k in range(4)
        )

    zero = jnp.zeros((4, 128), jnp.int32)
    found = lax.fori_loop(0, 128, invert, (zero,) * 4, unroll=4)
    slot_vec[...] = jnp.maximum(jnp.maximum(found[0], found[1]), jnp.maximum(found[2], found[3]))
    slot_copies = [
        pltpu.make_async_copy(slot_vec.at[t], slot_of.at[pl.ds(t * 128, 128)], load_sem.at[7 + t])
        for t in range(4)
    ]
    for copy in slot_copies:
        copy.start()

    loads[0].wait()
    for x in range(2, 5):
        for y in range(2, 5):
            for z in range(2, 5):
                raw[x * 49 + y * 7 + z] = jnp.zeros((2, 128), jnp.float32)

    def table_x(i, carry):
        t = [raw[x * 49 + i] for x in range(7)]
        vals = [t[1], t[3], t[5], t[2] - t[1], t[4] - t[3], t[6] - t[5]]
        vals += [t[0] - t[1], t[2] - t[3], t[4] - t[5]]
        for g, v in enumerate(vals):
            tab[i, g] = v
        return carry

    lax.fori_loop(0, 49, table_x, 0)

    def table_z(y, carry):
        def inner(g, carry):
            vals = line_kernel([tab[y * 7 + z, g] for z in range(7)])
            for fz, v in enumerate(vals):
                tab_z[y * F1 + fz, g] = v
            return carry

        return lax.fori_loop(0, 9, inner, carry, unroll=3)

    lax.fori_loop(0, 7, table_z, 0)

    def table_y(fz, carry):
        def inner(g, carry):
            vals = line_kernel([tab_z[y * F1 + fz, g] for y in range(7)])
            for fy, v in enumerate(vals):
                tab[fy * F1 + fz, g] = v
            return carry

        return lax.fori_loop(0, 9, inner, carry, unroll=3)

    lax.fori_loop(0, F1, table_y, 0)
    loads[2].wait()
    row = lax.broadcasted_iota(jnp.int32, (8, 128), 0)
    low = row < 4

    def chunk(i, carry):
        for copy in halo(i):
            copy.wait_recv()
        at = pl.ds(pl.multiple_of(i * rows, rows), rows)
        for c in range(4):
            parts = []
            if c < 2:
                parts.append((before, c * 128, (2 - c) * 128, 0))
            lo, hi = max(c, 2), min(c + 5, 6)
            parts.append((own, (lo - 2) * 128, (hi - lo) * 128, (lo - c) * 128))
            if c > 1:
                parts.append((after, 0, (c - 1) * 128, (6 - c) * 128))
            acc = None
            for ref, col, width, wrow in parts:
                piece = jnp.dot(
                    ref[at, pl.ds(col, width)],
                    weight[c, pl.ds(wrow, width), :],
                    preferred_element_type=jnp.float32,
                )
                acc = piece if acc is None else acc + piece
            total[...] = acc

            def tile_of(tile, carry, c=c):
                lane = pl.multiple_of(tile * 128, 128)
                wide = pl.multiple_of(c * 512 + tile * 128, 128)
                halves = [[], []]
                for k in range(2):
                    re = im = None
                    for h in range(8):
                        base = k * 128 + h * 16
                        ur = total[pl.ds(base, 8), pl.ds(lane, 128)]
                        ui = total[pl.ds(base + 8, 8), pl.ds(lane, 128)]
                        cs = jnp.broadcast_to(cosine[h : h + 1, pl.ds(wide, 128)], (8, 128))
                        sn = jnp.broadcast_to(sine[h : h + 1, pl.ds(wide, 128)], (8, 128))
                        r, m = cs * ur - sn * ui, sn * ur + cs * ui
                        re = r if re is None else re + r
                        im = m if im is None else im + m
                    keep = mask[2 * i + k]
                    re, im = re * keep, im * keep
                    halves[0].append(jnp.where(low, re, pltpu.roll(im, 4, 0)))
                    halves[1].append(jnp.where(low, pltpu.roll(re, 4, 0), im))
                for k in range(2):
                    value = jnp.concatenate(halves[k], axis=0).astype(jnp.bfloat16)
                    stage[(c * 4 + tile) * 2 + k, i] = value
                return carry

            lax.fori_loop(0, 4, tile_of, 0)
            for core in range(2):
                for z in range(4):
                    peer = c * 8 + ((bb // 2 + 2 + z) % 4) * 2 + (bb + core) % 2

                    @pl.when(peer != bb)
                    def _(peer=peer):
                        pltpu.make_async_remote_copy(
                            stage.at[peer, i], pats.at[bb * 8 + i], move_send, move_recv,
                            device_id={"box": peer},
                        ).start()

        return carry

    lax.fori_loop(0, CHUNKS, chunk, 0)
    mine = pltpu.make_async_copy(stage.at[bb], pats.at[pl.ds(bb * 8, 8)], local_sem)
    mine.start()
    pick = (row & 2) == 0

    def expand(fy, carry):
        def inner(fz, carry):
            for g in range(9):
                here, there = tab.at[fy * F1 + fz, g], tab.at[fy * F1 + fz + 9, g]
                two = []
                for part in range(2):
                    left = jnp.broadcast_to(here[part : part + 1, :], (8, 128))
                    right = jnp.broadcast_to(there[part : part + 1, :], (8, 128))
                    two.append(jnp.where(pick, left, right))
                tiles[fy * 9 + fz, g, 0] = two[0]
                tiles[fy * 9 + fz, g, 1] = jnp.where(low, -two[1], two[1])
            return carry

        return lax.fori_loop(0, 9, inner, carry)

    lax.fori_loop(0, F1, expand, 0)
    for copy in slot_copies:
        copy.wait()
    mine.wait()
    pltpu.make_async_copy(pats.at[pl.ds(0, 248)], pats.at[pl.ds(0, 248)], move_recv).wait()

    def widen(i, carry):
        both = pats[i].astype(jnp.float32)
        wide_x[2 * i] = both[0:8]
        wide_x[2 * i + 1] = both[8:16]
        return carry

    lax.fori_loop(0, 256, widen, 0, unroll=8)

    for half in range(2):

        def in_z(i, carry):
            vals = []
            for z in range(8):
                at = i * 8 + z
                if half == 0:
                    left, right = wide_x[slot_of[at]], wide_x[slot_of[at + 256]]
                    vals.append(jnp.where(pick, left, pltpu.roll(right, 2, 0)))
                    later[at] = jnp.where(pick, pltpu.roll(left, 6, 0), right)
                else:
                    vals.append(later[at])
            vals = line_in(vals)
            for fz in range(9):
                left, right = vals[fz], vals[fz + 9]
                lines[i * 9 + fz] = jnp.where(pick, left, pltpu.roll(right, 2, 0))
                lines[(i + 32) * 9 + fz] = jnp.where(pick, pltpu.roll(left, 6, 0), right)
            return carry

        lax.fori_loop(0, 32, in_z, 0, unroll=4)

        def in_y(x, carry):
            def inner(fz, carry):
                vals = line_in([lines[(x * 8 + y) * 9 + fz] for y in range(8)])
                for fy, v in enumerate(vals):
                    spec[fy * 9 + fz, x] = v
                return carry

            return lax.fori_loop(0, 9, inner, carry, unroll=3)

        lax.fori_loop(0, 8, in_y, 0)

        def product(f, carry):
            src = [spec[f, x] for x in range(8)]
            turn = [pltpu.roll(v, 4, 0) for v in src]
            sets = [
                ([src[2 * j] + src[2 * j + 1] for j in range(4)], [turn[2 * j] + turn[2 * j + 1] for j in range(4)]),
                (src[1::2], turn[1::2]),
                (src[0::2], turn[0::2]),
            ]
            sums = []
            for g, (x, t) in enumerate(sets):
                acc = [None] * 4
                for j in range(-1, 2):
                    a, b = tiles[f, g * 3 + j + 1, 0], tiles[f, g * 3 + j + 1, 1]
                    for i in range(4):
                        if 0 <= i + j < 4:
                            v = a * x[i + j] + b * t[i + j]
                            acc[i] = v if acc[i] is None else acc[i] + v
                sums.append(acc)
            for i in range(4):
                spec[f, 2 * i] = sums[0][i] + sums[1][i]
                spec[f, 2 * i + 1] = sums[0][i] + sums[2][i]
            return carry

        lax.fori_loop(0, NF // 2, product, 0, unroll=9)

        def out_y(x, carry):
            def inner(fz, carry):
                vals = line_out([spec[fy * 9 + fz, x] for fy in range(F1)])
                for y, v in enumerate(vals):
                    lines[(x * 8 + y) * 9 + fz] = v
                return carry

            return lax.fori_loop(0, 9, inner, carry, unroll=3)

        lax.fori_loop(0, 8, out_y, 0)

        def out_z(i, carry):
            near, away = [], []
            for fz in range(9):
                left, right = lines[i * 9 + fz], lines[(i + 32) * 9 + fz]
                near.append(jnp.where(pick, left, pltpu.roll(right, 2, 0)))
                away.append(jnp.where(pick, pltpu.roll(left, 6, 0), right))
            for z, v in enumerate(line_out(near + away)):
                grid_x[i * 8 + z] = v
                grid_x[256 + i * 8 + z] = pltpu.roll(v, 6, 0)
            return carry

        lax.fori_loop(0, 32, out_z, 0, unroll=2)

        def give(target, half=half):
            for q in range(4):
                vals = [grid_x[slot_parent[target * 16 + 4 * q + k]] for k in range(4)]
                pairs = [jnp.where(pick, vals[k], pltpu.roll(vals[k + 1], 2, 0)) for k in (0, 2)]
                back[half, target, q] = jnp.concatenate(pairs, axis=0).astype(jnp.bfloat16)

        for peer in peers:
            give(peer)
            pltpu.make_async_remote_copy(
                back.at[half, peer], out.at[half, bb], back_send.at[half], back_recv.at[half],
                device_id={"box": peer},
            ).start()
        give(bb)
        pltpu.make_async_copy(back.at[half, bb], out.at[half, bb], home_sem.at[half]).start()

    for i in range(CHUNKS):
        for copy in halo(i):
            copy.wait_send()
    most = pl.ds(0, 31)
    pltpu.make_async_copy(stage.at[most], stage.at[most], move_send).wait()
    for half in range(2):
        pltpu.make_async_copy(back.at[half, bb], out.at[half, bb], home_sem.at[half]).wait()
        sent, got = back.at[half, most], out.at[half, most]
        pltpu.make_async_copy(sent, sent, back_send.at[half]).wait()
        pltpu.make_async_copy(got, got, back_recv.at[half]).wait()


def far_pieces(child, interp, blocks, angle, slot_parent, far, trans):
    any_space = pl.BlockSpec(memory_space=pl.ANY)
    return pl.pallas_call(
        main_kernel,
        in_specs=[any_space] * 7,
        out_specs=any_space,
        out_shape=jax.ShapeDtypeStruct((2, 32, 4, 16, 128), jnp.bfloat16),
        scratch_shapes=[
            pltpu.VMEM((2048, 512), jnp.bfloat16),
            pltpu.VMEM((2048, 256), jnp.bfloat16),
            pltpu.VMEM((2048, 256), jnp.bfloat16),
            pltpu.VMEM((16, 4, 128, 128), jnp.bfloat16),
            pltpu.VMEM((4, 640, 512), jnp.bfloat16),
            pltpu.VMEM((2048 // CHUNKS, 512), jnp.float32),
            pltpu.VMEM((32, 8, 16, 128), jnp.bfloat16),
            pltpu.VMEM((8, 2048), jnp.float32),
            pltpu.VMEM((8, 2048), jnp.float32),
            pltpu.VMEM((343, 2, 128), jnp.float32),
            pltpu.VMEM((7 * F1, 9, 2, 128), jnp.float32),
            pltpu.VMEM((NF, 9, 2, 128), jnp.float32),
            pltpu.VMEM((NF // 2, 9, 2, 8, 128), jnp.float32),
            pltpu.VMEM((189, 512), jnp.int32),
            pltpu.VMEM((4, 128), jnp.float32),
            pltpu.VMEM((16, 8, 128), jnp.float32),
            pltpu.VMEM((4, 128), jnp.int32),
            pltpu.SMEM((512,), jnp.int32),
            pltpu.SMEM((512,), jnp.int32),
            pltpu.SMEM((4, 16), jnp.int32),
            pltpu.VMEM((8, 2048), jnp.float32),
            pltpu.VMEM((256, 16, 128), jnp.bfloat16),
            pltpu.VMEM((512, 8, 128), jnp.float32),
            pltpu.VMEM((256, 8, 128), jnp.float32),
            pltpu.VMEM((512, 8, 128), jnp.float32),
            pltpu.VMEM((32 * F1, 8, 128), jnp.float32),
            pltpu.VMEM((NF // 2, 8, 8, 128), jnp.float32),
            pltpu.VMEM((2, 32, 4, 16, 128), jnp.bfloat16),
            pltpu.SemaphoreType.DMA((11,)),
            pltpu.SemaphoreType.DMA((2, CHUNKS)),
            pltpu.SemaphoreType.DMA((2, CHUNKS)),
            pltpu.SemaphoreType.DMA,
            pltpu.SemaphoreType.DMA,
            pltpu.SemaphoreType.DMA,
            pltpu.SemaphoreType.DMA((2,)),
            pltpu.SemaphoreType.DMA((2,)),
            pltpu.SemaphoreType.DMA((2,)),
        ],
        compiler_params=pltpu.CompilerParams(collective_id=0, has_side_effects=True, vmem_limit_bytes=46 * 2**20),
    )(*[pltpu.with_memory_space_constraint(v, pltpu.HBM) for v in (child, interp, blocks, angle, slot_parent, far, trans)])


def arrange_kernel(src, dst, got, out, in_sem, out_sem):
    row = lax.broadcasted_iota(jnp.int32, (8, 128), 0)
    low, pick = row < 4, (row & 2) == 0

    def swap(a, b, mask, shift):
        return (
            jnp.where(mask, a, pltpu.roll(b, shift, 0)),
            jnp.where(mask, pltpu.roll(a, 8 - shift, 0), b),
        )

    fetch = [pltpu.make_async_copy(src.at[:, :, n], got.at[n], in_sem.at[n]) for n in range(4)]
    store = [pltpu.make_async_copy(out.at[pl.ds(4 * n, 4)], dst.at[pl.ds(4 * n, 4)], out_sem.at[n]) for n in range(4)]
    for copy in fetch:
        copy.start()
    for n in range(4):
        fetch[n].wait()
        for c in range(16):
            parts = [got[n, half, 2 * c + odd].astype(jnp.float32) for odd in range(2) for half in range(2)]
            lanes = slice(c * 128, c * 128 + 128)
            for k in range(2):
                v0, v1, v2, v3 = [v[8 * k : 8 * k + 8] for v in parts]
                p, r = swap(v0, v2, low, 4)
                q, s = swap(v1, v3, low, 4)
                at = 4 * n + 2 * k
                out[at, 0, :, lanes], out[at + 1, 0, :, lanes] = swap(p, q, pick, 2)
                out[at, 1, :, lanes], out[at + 1, 1, :, lanes] = swap(r, s, pick, 2)
        store[n].start()
    for copy in store:
        copy.wait()


def arrange(got):
    return pl.pallas_call(
        arrange_kernel,
        in_specs=[pl.BlockSpec(memory_space=pl.ANY)],
        out_specs=pl.BlockSpec(memory_space=pl.ANY),
        out_shape=jax.ShapeDtypeStruct((16, 2, 8, 2048), jnp.float32),
        scratch_shapes=[
            pltpu.VMEM((4, 2, 32, 16, 128), jnp.bfloat16),
            pltpu.VMEM((16, 2, 8, 2048), jnp.float32),
            pltpu.SemaphoreType.DMA((4,)),
            pltpu.SemaphoreType.DMA((4,)),
        ],
        compiler_params=pltpu.CompilerParams(vmem_limit_bytes=8 * 2**20),
    )(got)


def shards(child_pat, interp, interp_blocks, shift_angle, slot_parent, far_list, trans):
    pieces = far_pieces(
        child_pat.reshape(2048, 512),
        interp,
        interp_blocks.T,
        shift_angle,
        slot_parent,
        far_list.T,
        jnp.transpose(trans, (1, 0, 2)),
    )
    return arrange(pieces)


def solution(mesh):
    in_specs = (
        P("box", None, None, "dir"),
        P("dir", None, None, None),
        P("dir", None),
        P(None, "dir"),
        P(),
        P(),
        P(None, None, "dir"),
    )
    out_specs = P("box", None, None, "dir")
    return jax.shard_map(shards, mesh=mesh, in_specs=in_specs, out_specs=out_specs, check_vma=False)
```

```python
import jax
import jax.numpy as jnp
from jax import lax
from jax.experimental import pallas as pl
from jax.experimental.pallas import tpu as pltpu
from jax.sharding import PartitionSpec as P

G = 8
F1 = 18
NF = F1 * F1


def toom_in(v):
    a, b = v[0] + v[2], v[1] + v[3]
    c, d = v[0] + 4.0 * v[2], 2.0 * v[1] + 8.0 * v[3]
    return [v[0], v[3], a + b, a - b, c + d, c - d]


def line_in(x):
    even, odd = x[0::2], x[1::2]
    both = [e + o for e, o in zip(even, odd)]
    return toom_in(both) + toom_in(odd) + toom_in(even)


def toom_kernel(k):
    h2, h1, h0 = k
    a, b = (h0 + h2) * 0.5, h1 * 0.5
    c, d = (h0 + 4.0 * h2) * (1.0 / 24.0), h1 * (1.0 / 12.0)
    return [h0, h2, a + b, a - b, c + d, c - d]


def line_kernel(t):
    k0 = [t[1], t[3], t[5]]
    up = [t[2] - t[1], t[4] - t[3], t[6] - t[5]]
    down = [t[0] - t[1], t[2] - t[3], t[4] - t[5]]
    return toom_kernel(k0) + toom_kernel(up) + toom_kernel(down)


def toom_out(m):
    z0, z5 = m[0], m[1]
    e1, o1 = m[2] + m[3], m[2] - m[3]
    e2, d2 = m[4] + m[5], m[4] - m[5]
    z4 = e2 - e1 * (1.0 / 3.0) + z0 * 0.25
    z2 = e1 - z0 - z4
    z3 = 2.0 * d2 - o1 * (1.0 / 3.0) - 5.0 * z5
    z1 = o1 - z3 - z5
    return [z1, z2, z3, z4]


def line_out(m):
    base, up, down = toom_out(m[0:6]), toom_out(m[6:12]), toom_out(m[12:18])
    out = []
    for i in range(4):
        out += [base[i] + up[i], base[i] + down[i]]
    return out


TURNS = [(2, 2), (1, 2), (2, 1), (3, 2), (2, 3), (1, 1), (3, 1), (3, 3), (1, 3), (2, 0), (0, 2), (1, 0), (0, 1), (3, 0), (0, 3)]
PEERS = [(x, z, c) for x, z in TURNS for c in range(2)] + [(0, 0, 1)]
CHUNKS = 8


def peers_of(bb):
    x, z, c = bb // 8, (bb // 2) % 4, bb % 2
    return [((x + dx) % 4) * 8 + ((z + dz) % 4) * 2 + (c + dc) % 2 for dx, dz, dc in PEERS]


def main_kernel(
    child, interp, blocks_in, angle_in, slot_in, far, trans, out,
    own, before, after, weights, weight, total, stage, cosine, sine, raw, tab_z, tab, tiles,
    listed, occ, mask, slot_vec, slot_of, slot_parent, blocks, angle,
    pats, wide_x, later, grid_x, lines, spec, back,
    load_sem, halo_send, halo_recv, move_send, move_recv, local_sem, home_sem, back_send, back_recv,
):
    bb, dd = lax.axis_index("box"), lax.axis_index("dir")
    dirs = lax.axis_size("dir")
    rows = 2048 // CHUNKS
    peers = peers_of(bb)
    above, below = (dd + 1) % dirs, (dd + dirs - 1) % dirs
    barrier = pltpu.get_barrier_semaphore()
    pl.semaphore_signal(barrier, 1, device_id={"dir": above})
    pl.semaphore_signal(barrier, 1, device_id={"dir": below})
    for peer in peers:
        pl.semaphore_signal(barrier, 1, device_id={"box": peer})
    first = pl.multiple_of((bb // 2) * 128, 128)
    loads = [
        pltpu.make_async_copy(trans.at[:, :, pl.ds(first, 128)], raw, load_sem.at[0]),
        pltpu.make_async_copy(interp, weights, load_sem.at[1]),
        pltpu.make_async_copy(child, own, load_sem.at[2]),
        pltpu.make_async_copy(far, listed, load_sem.at[3]),
        pltpu.make_async_copy(blocks_in, blocks, load_sem.at[4]),
        pltpu.make_async_copy(slot_in, slot_parent, load_sem.at[5]),
        pltpu.make_async_copy(angle_in, angle, load_sem.at[6]),
    ]
    for copy in loads:
        copy.start()
    pl.semaphore_wait(barrier, len(peers) + 2)

    def halo(i):
        at = pl.ds(pl.multiple_of(i * rows, rows), rows)
        return [
            pltpu.make_async_remote_copy(
                child.at[at, pl.ds(256, 256)], before.at[at, :],
                halo_send.at[0, i], halo_recv.at[0, i], device_id={"dir": above},
            ),
            pltpu.make_async_remote_copy(
                child.at[at, pl.ds(0, 256)], after.at[at, :],
                halo_send.at[1, i], halo_recv.at[1, i], device_id={"dir": below},
            ),
        ]

    for i in range(CHUNKS):
        for copy in halo(i):
            copy.start()

    loads[6].wait()
    cosine[...] = jnp.cos(angle[...])
    sine[...] = jnp.sin(angle[...])
    loads[1].wait()
    loads[4].wait()
    for j in range(16):
        rel = [(blocks[b, j] - (dd * 4 + j // 4) + 18) & 15 for b in range(4)]
        for o in range(5):
            value = None
            for b in (o - 1, o):
                if 0 <= b < 4:
                    term = weights[j, b].astype(jnp.float32) * jnp.where(rel[b] == o, 1.0, 0.0)
                    value = term if value is None else value + term
            lanes = pl.ds((j % 4) * 128, 128)
            weight[j // 4, pl.ds(o * 128, 128), lanes] = value.astype(jnp.bfloat16)

    loads[3].wait()
    loads[5].wait()
    lane = lax.broadcasted_iota(jnp.int32, (189, 128), 1)
    for t in range(4):
        watch = listed[:, pl.ds((t + 1 if t < 3 else 2) * 128, 128)]
        occ[t : t + 1, :] = jnp.max(jnp.where(watch == lane + t * 128, 1.0, 0.0), axis=0, keepdims=True)
    ident = lax.broadcasted_iota(jnp.int32, (4, 128), 0) * 128 + lax.broadcasted_iota(jnp.int32, (4, 128), 1)
    for s in range(16):
        held = jnp.where(ident == slot_parent[bb * 16 + s], occ[...], 0.0)
        held = jnp.max(jnp.max(held, axis=1, keepdims=True), axis=0, keepdims=True)
        mask[s] = jnp.broadcast_to(held, (8, 128))

    def invert(i, found):
        return tuple(
            jnp.where(ident == slot_parent[i * 4 + k], i * 4 + k, found[k]) for k in range(4)
        )

    zero = jnp.zeros((4, 128), jnp.int32)
    found = lax.fori_loop(0, 128, invert, (zero,) * 4, unroll=4)
    slot_vec[...] = jnp.maximum(jnp.maximum(found[0], found[1]), jnp.maximum(found[2], found[3]))
    slot_copies = [
        pltpu.make_async_copy(slot_vec.at[t], slot_of.at[pl.ds(t * 128, 128)], load_sem.at[7 + t])
        for t in range(4)
    ]
    for copy in slot_copies:
        copy.start()

    loads[0].wait()
    for x in range(2, 5):
        for y in range(2, 5):
            for z in range(2, 5):
                raw[x * 49 + y * 7 + z] = jnp.zeros((2, 128), jnp.float32)

    def table_x(i, carry):
        t = [raw[x * 49 + i] for x in range(7)]
        vals = [t[1], t[3], t[5], t[2] - t[1], t[4] - t[3], t[6] - t[5]]
        vals += [t[0] - t[1], t[2] - t[3], t[4] - t[5]]
        for g, v in enumerate(vals):
            tab[i, g] = v
        return carry

    lax.fori_loop(0, 49, table_x, 0)

    def table_z(y, carry):
        def inner(g, carry):
            vals = line_kernel([tab[y * 7 + z, g] for z in range(7)])
            for fz, v in enumerate(vals):
                tab_z[y * F1 + fz, g] = v
            return carry

        return lax.fori_loop(0, 9, inner, carry, unroll=3)

    lax.fori_loop(0, 7, table_z, 0)

    def table_y(fz, carry):
        def inner(g, carry):
            vals = line_kernel([tab_z[y * F1 + fz, g] for y in range(7)])
            for fy, v in enumerate(vals):
                tab[fy * F1 + fz, g] = v
            return carry

        return lax.fori_loop(0, 9, inner, carry, unroll=3)

    lax.fori_loop(0, F1, table_y, 0)
    loads[2].wait()
    row = lax.broadcasted_iota(jnp.int32, (8, 128), 0)
    low = row < 4

    def chunk(i, carry):
        for copy in halo(i):
            copy.wait_recv()
        at = pl.ds(pl.multiple_of(i * rows, rows), rows)
        for c in range(4):
            parts = []
            if c < 2:
                parts.append((before, c * 128, (2 - c) * 128, 0))
            lo, hi = max(c, 2), min(c + 5, 6)
            parts.append((own, (lo - 2) * 128, (hi - lo) * 128, (lo - c) * 128))
            if c > 1:
                parts.append((after, 0, (c - 1) * 128, (6 - c) * 128))
            acc = None
            for ref, col, width, wrow in parts:
                piece = jnp.dot(
                    ref[at, pl.ds(col, width)],
                    weight[c, pl.ds(wrow, width), :],
                    preferred_element_type=jnp.float32,
                )
                acc = piece if acc is None else acc + piece
            total[c % 2] = acc

            def tile_of(tile, carry, c=c):
                lane = tile * 128
                wide = c * 512 + tile * 128
                halves = [[], []]
                for k in range(2):
                    re = im = None
                    for h in range(8):
                        base = k * 128 + h * 16
                        ur = total[c % 2, pl.ds(base, 8), pl.ds(lane, 128)]
                        ui = total[c % 2, pl.ds(base + 8, 8), pl.ds(lane, 128)]
                        cs = jnp.broadcast_to(cosine[h : h + 1, pl.ds(wide, 128)], (8, 128))
                        sn = jnp.broadcast_to(sine[h : h + 1, pl.ds(wide, 128)], (8, 128))
                        r, m = cs * ur - sn * ui, sn * ur + cs * ui
                        re = r if re is None else re + r
                        im = m if im is None else im + m
                    keep = mask[2 * i + k]
                    re, im = re * keep, im * keep
                    halves[0].append(jnp.where(low, re, pltpu.roll(im, 4, 0)))
                    halves[1].append(jnp.where(low, pltpu.roll(re, 4, 0), im))
                for k in range(2):
                    value = jnp.concatenate(halves[k], axis=0).astype(jnp.bfloat16)
                    stage[(c * 4 + tile) * 2 + k, i] = value
                return carry

            for tile in range(4):
                tile_of(tile, 0)
        for peer in peers:
            pltpu.make_async_remote_copy(
                stage.at[peer, i], pats.at[bb * 8 + i], move_send, move_recv,
                device_id={"box": peer},
            ).start()
        return carry

    lax.fori_loop(0, CHUNKS, chunk, 0)
    mine = pltpu.make_async_copy(stage.at[bb], pats.at[pl.ds(bb * 8, 8)], local_sem)
    mine.start()
    pick = (row & 2) == 0

    def expand(fy, carry):
        def inner(fz, carry):
            for g in range(9):
                here, there = tab.at[fy * F1 + fz, g], tab.at[fy * F1 + fz + 9, g]
                two = []
                for part in range(2):
                    left = jnp.broadcast_to(here[part : part + 1, :], (8, 128))
                    right = jnp.broadcast_to(there[part : part + 1, :], (8, 128))
                    two.append(jnp.where(pick, left, right))
                tiles[fy * 9 + fz, g, 0] = two[0]
                tiles[fy * 9 + fz, g, 1] = jnp.where(low, -two[1], two[1])
            return carry

        return lax.fori_loop(0, 9, inner, carry)

    lax.fori_loop(0, F1, expand, 0)
    for copy in slot_copies:
        copy.wait()
    mine.wait()
    pltpu.make_async_copy(pats.at[pl.ds(0, 248)], pats.at[pl.ds(0, 248)], move_recv).wait()

    def widen(i, carry):
        both = pats[i].astype(jnp.float32)
        wide_x[2 * i] = both[0:8]
        wide_x[2 * i + 1] = both[8:16]
        return carry

    lax.fori_loop(0, 256, widen, 0, unroll=8)

    for half in range(2):

        def in_z(i, carry):
            vals = []
            for z in range(8):
                at = i * 8 + z
                if half == 0:
                    left, right = wide_x[slot_of[at]], wide_x[slot_of[at + 256]]
                    vals.append(jnp.where(pick, left, pltpu.roll(right, 2, 0)))
                    later[at] = jnp.where(pick, pltpu.roll(left, 6, 0), right)
                else:
                    vals.append(later[at])
            vals = line_in(vals)
            for fz in range(9):
                left, right = vals[fz], vals[fz + 9]
                lines[i * 9 + fz] = jnp.where(pick, left, pltpu.roll(right, 2, 0))
                lines[(i + 32) * 9 + fz] = jnp.where(pick, pltpu.roll(left, 6, 0), right)
            return carry

        lax.fori_loop(0, 32, in_z, 0, unroll=8)

        def in_y(x, carry):
            def inner(fz, carry):
                vals = line_in([lines[(x * 8 + y) * 9 + fz] for y in range(8)])
                for fy, v in enumerate(vals):
                    spec[fy * 9 + fz, x] = v
                return carry

            return lax.fori_loop(0, 9, inner, carry, unroll=9)

        lax.fori_loop(0, 8, in_y, 0)

        def product(f, carry):
            src = [spec[f, x] for x in range(8)]
            turn = [pltpu.roll(v, 4, 0) for v in src]
            sets = [
                ([src[2 * j] + src[2 * j + 1] for j in range(4)], [turn[2 * j] + turn[2 * j + 1] for j in range(4)]),
                (src[1::2], turn[1::2]),
                (src[0::2], turn[0::2]),
            ]
            sums = []
            for g, (x, t) in enumerate(sets):
                acc = [None] * 4
                for j in range(-1, 2):
                    a, b = tiles[f, g * 3 + j + 1, 0], tiles[f, g * 3 + j + 1, 1]
                    for i in range(4):
                        if 0 <= i + j < 4:
                            v = a * x[i + j] + b * t[i + j]
                            acc[i] = v if acc[i] is None else acc[i] + v
                sums.append(acc)
            for i in range(4):
                spec[f, 2 * i] = sums[0][i] + sums[1][i]
                spec[f, 2 * i + 1] = sums[0][i] + sums[2][i]
            return carry

        lax.fori_loop(0, NF // 2, product, 0, unroll=18)

        def out_y(x, carry):
            def inner(fz, carry):
                vals = line_out([spec[fy * 9 + fz, x] for fy in range(F1)])
                for y, v in enumerate(vals):
                    lines[(x * 8 + y) * 9 + fz] = v
                return carry

            return lax.fori_loop(0, 9, inner, carry, unroll=9)

        lax.fori_loop(0, 8, out_y, 0)

        def out_z(i, carry):
            near, away = [], []
            for fz in range(9):
                left, right = lines[i * 9 + fz], lines[(i + 32) * 9 + fz]
                near.append(jnp.where(pick, left, pltpu.roll(right, 2, 0)))
                away.append(jnp.where(pick, pltpu.roll(left, 6, 0), right))
            for z, v in enumerate(line_out(near + away)):
                grid_x[i * 8 + z] = v
                grid_x[256 + i * 8 + z] = pltpu.roll(v, 6, 0)
            return carry

        lax.fori_loop(0, 32, out_z, 0, unroll=8)

        def give(target, half=half):
            for q in range(4):
                vals = [grid_x[slot_parent[target * 16 + 4 * q + k]] for k in range(4)]
                pairs = [jnp.where(pick, vals[k], pltpu.roll(vals[k + 1], 2, 0)) for k in (0, 2)]
                back[half, target, q] = jnp.concatenate(pairs, axis=0).astype(jnp.bfloat16)

        for peer in peers:
            give(peer)
            pltpu.make_async_remote_copy(
                back.at[half, peer], out.at[half, bb], back_send.at[half], back_recv.at[half],
                device_id={"box": peer},
            ).start()
        give(bb)
        pltpu.make_async_copy(back.at[half, bb], out.at[half, bb], home_sem.at[half]).start()

    for i in range(CHUNKS):
        for copy in halo(i):
            copy.wait_send()
    most = pl.ds(0, 31)
    pltpu.make_async_copy(stage.at[most], stage.at[most], move_send).wait()
    for half in range(2):
        pltpu.make_async_copy(back.at[half, bb], out.at[half, bb], home_sem.at[half]).wait()
        sent, got = back.at[half, most], out.at[half, most]
        pltpu.make_async_copy(sent, sent, back_send.at[half]).wait()
        pltpu.make_async_copy(got, got, back_recv.at[half]).wait()


def far_pieces(child, interp, blocks, angle, slot_parent, far, trans):
    any_space = pl.BlockSpec(memory_space=pl.ANY)
    return pl.pallas_call(
        main_kernel,
        in_specs=[any_space] * 7,
        out_specs=any_space,
        out_shape=jax.ShapeDtypeStruct((2, 32, 4, 16, 128), jnp.bfloat16),
        scratch_shapes=[
            pltpu.VMEM((2048, 512), jnp.bfloat16),
            pltpu.VMEM((2048, 256), jnp.bfloat16),
            pltpu.VMEM((2048, 256), jnp.bfloat16),
            pltpu.VMEM((16, 4, 128, 128), jnp.bfloat16),
            pltpu.VMEM((4, 640, 512), jnp.bfloat16),
            pltpu.VMEM((2, 2048 // CHUNKS, 512), jnp.float32),
            pltpu.VMEM((32, 8, 16, 128), jnp.bfloat16),
            pltpu.VMEM((8, 2048), jnp.float32),
            pltpu.VMEM((8, 2048), jnp.float32),
            pltpu.VMEM((343, 2, 128), jnp.float32),
            pltpu.VMEM((7 * F1, 9, 2, 128), jnp.float32),
            pltpu.VMEM((NF, 9, 2, 128), jnp.float32),
            pltpu.VMEM((NF // 2, 9, 2, 8, 128), jnp.float32),
            pltpu.VMEM((189, 512), jnp.int32),
            pltpu.VMEM((4, 128), jnp.float32),
            pltpu.VMEM((16, 8, 128), jnp.float32),
            pltpu.VMEM((4, 128), jnp.int32),
            pltpu.SMEM((512,), jnp.int32),
            pltpu.SMEM((512,), jnp.int32),
            pltpu.SMEM((4, 16), jnp.int32),
            pltpu.VMEM((8, 2048), jnp.float32),
            pltpu.VMEM((256, 16, 128), jnp.bfloat16),
            pltpu.VMEM((512, 8, 128), jnp.float32),
            pltpu.VMEM((256, 8, 128), jnp.float32),
            pltpu.VMEM((512, 8, 128), jnp.float32),
            pltpu.VMEM((32 * F1, 8, 128), jnp.float32),
            pltpu.VMEM((NF // 2, 8, 8, 128), jnp.float32),
            pltpu.VMEM((2, 32, 4, 16, 128), jnp.bfloat16),
            pltpu.SemaphoreType.DMA((11,)),
            pltpu.SemaphoreType.DMA((2, CHUNKS)),
            pltpu.SemaphoreType.DMA((2, CHUNKS)),
            pltpu.SemaphoreType.DMA,
            pltpu.SemaphoreType.DMA,
            pltpu.SemaphoreType.DMA,
            pltpu.SemaphoreType.DMA((2,)),
            pltpu.SemaphoreType.DMA((2,)),
            pltpu.SemaphoreType.DMA((2,)),
        ],
        compiler_params=pltpu.CompilerParams(collective_id=0, has_side_effects=True, vmem_limit_bytes=46 * 2**20),
    )(*[pltpu.with_memory_space_constraint(v, pltpu.HBM) for v in (child, interp, blocks, angle, slot_parent, far, trans)])


def arrange_kernel(src, dst, got, out, in_sem, out_sem):
    row = lax.broadcasted_iota(jnp.int32, (8, 128), 0)
    low, pick = row < 4, (row & 2) == 0

    def swap(a, b, mask, shift):
        return (
            jnp.where(mask, a, pltpu.roll(b, shift, 0)),
            jnp.where(mask, pltpu.roll(a, 8 - shift, 0), b),
        )

    fetch = [pltpu.make_async_copy(src.at[:, :, n], got.at[n], in_sem.at[n]) for n in range(4)]
    store = [pltpu.make_async_copy(out.at[pl.ds(4 * n, 4)], dst.at[pl.ds(4 * n, 4)], out_sem.at[n]) for n in range(4)]
    for copy in fetch:
        copy.start()
    for n in range(4):
        fetch[n].wait()
        for c in range(16):
            parts = [got[n, half, 2 * c + odd].astype(jnp.float32) for odd in range(2) for half in range(2)]
            lanes = slice(c * 128, c * 128 + 128)
            for k in range(2):
                v0, v1, v2, v3 = [v[8 * k : 8 * k + 8] for v in parts]
                p, r = swap(v0, v2, low, 4)
                q, s = swap(v1, v3, low, 4)
                at = 4 * n + 2 * k
                out[at, 0, :, lanes], out[at + 1, 0, :, lanes] = swap(p, q, pick, 2)
                out[at, 1, :, lanes], out[at + 1, 1, :, lanes] = swap(r, s, pick, 2)
        store[n].start()
    for copy in store:
        copy.wait()


def arrange(got):
    return pl.pallas_call(
        arrange_kernel,
        in_specs=[pl.BlockSpec(memory_space=pl.ANY)],
        out_specs=pl.BlockSpec(memory_space=pl.ANY),
        out_shape=jax.ShapeDtypeStruct((16, 2, 8, 2048), jnp.float32),
        scratch_shapes=[
            pltpu.VMEM((4, 2, 32, 16, 128), jnp.bfloat16),
            pltpu.VMEM((16, 2, 8, 2048), jnp.float32),
            pltpu.SemaphoreType.DMA((4,)),
            pltpu.SemaphoreType.DMA((4,)),
        ],
        compiler_params=pltpu.CompilerParams(vmem_limit_bytes=8 * 2**20),
    )(got)


def shards(child_pat, interp, interp_blocks, shift_angle, slot_parent, far_list, trans):
    pieces = far_pieces(
        child_pat.reshape(2048, 512),
        interp,
        interp_blocks.T,
        shift_angle,
        slot_parent,
        far_list.T,
        jnp.transpose(trans, (1, 0, 2)),
    )
    return arrange(pieces)


def solution(mesh):
    in_specs = (
        P("box", None, None, "dir"),
        P("dir", None, None, None),
        P("dir", None),
        P(None, "dir"),
        P(),
        P(),
        P(None, None, "dir"),
    )
    out_specs = P("box", None, None, "dir")
    return jax.shard_map(shards, mesh=mesh, in_specs=in_specs, out_specs=out_specs, check_vma=False)
```

```python
import jax
import jax.numpy as jnp
from jax import lax
from jax.experimental import pallas as pl
from jax.experimental.pallas import tpu as pltpu
from jax.sharding import PartitionSpec as P

G = 8
F1 = 18
NF = F1 * F1


def toom_in(v):
    a, b = v[0] + v[2], v[1] + v[3]
    c, d = v[0] + 4.0 * v[2], 2.0 * v[1] + 8.0 * v[3]
    return [v[0], v[3], a + b, a - b, c + d, c - d]


def line_in(x):
    even, odd = x[0::2], x[1::2]
    both = [e + o for e, o in zip(even, odd)]
    return toom_in(both) + toom_in(odd) + toom_in(even)


def toom_kernel(k):
    h2, h1, h0 = k
    a, b = (h0 + h2) * 0.5, h1 * 0.5
    c, d = (h0 + 4.0 * h2) * (1.0 / 24.0), h1 * (1.0 / 12.0)
    return [h0, h2, a + b, a - b, c + d, c - d]


def line_kernel(t):
    k0 = [t[1], t[3], t[5]]
    up = [t[2] - t[1], t[4] - t[3], t[6] - t[5]]
    down = [t[0] - t[1], t[2] - t[3], t[4] - t[5]]
    return toom_kernel(k0) + toom_kernel(up) + toom_kernel(down)


def toom_out(m):
    z0, z5 = m[0], m[1]
    e1, o1 = m[2] + m[3], m[2] - m[3]
    e2, d2 = m[4] + m[5], m[4] - m[5]
    z4 = e2 - e1 * (1.0 / 3.0) + z0 * 0.25
    z2 = e1 - z0 - z4
    z3 = 2.0 * d2 - o1 * (1.0 / 3.0) - 5.0 * z5
    z1 = o1 - z3 - z5
    return [z1, z2, z3, z4]


def line_out(m):
    base, up, down = toom_out(m[0:6]), toom_out(m[6:12]), toom_out(m[12:18])
    out = []
    for i in range(4):
        out += [base[i] + up[i], base[i] + down[i]]
    return out


TURNS = [(2, 2), (1, 2), (2, 1), (3, 2), (2, 3), (1, 1), (3, 1), (3, 3), (1, 3), (2, 0), (0, 2), (1, 0), (0, 1), (3, 0), (0, 3)]
PEERS = [(x, z, c) for x, z in TURNS for c in range(2)] + [(0, 0, 1)]
CHUNKS = 16


def peers_of(bb):
    x, z, c = bb // 8, (bb // 2) % 4, bb % 2
    return [((x + dx) % 4) * 8 + ((z + dz) % 4) * 2 + (c + dc) % 2 for dx, dz, dc in PEERS]


def main_kernel(
    child, interp, blocks_in, angle_in, slot_in, far, trans, out,
    own, before, after, weights, weight, total, stage, cosine, sine, raw, tab_z, tab, tiles,
    listed, occ, mask, slot_vec, slot_of, slot_parent, blocks, angle,
    pats, later, grid_x, lines, spec, back,
    load_sem, halo_send, halo_recv, move_send, move_recv, local_sem, home_sem, back_send, back_recv,
):
    bb, dd = lax.axis_index("box"), lax.axis_index("dir")
    dirs = lax.axis_size("dir")
    rows = 2048 // CHUNKS
    peers = peers_of(bb)
    above, below = (dd + 1) % dirs, (dd + dirs - 1) % dirs
    barrier = pltpu.get_barrier_semaphore()
    pl.semaphore_signal(barrier, 1, device_id={"dir": above})
    pl.semaphore_signal(barrier, 1, device_id={"dir": below})
    for peer in peers:
        pl.semaphore_signal(barrier, 1, device_id={"box": peer})
    first = pl.multiple_of((bb // 2) * 128, 128)
    loads = [
        pltpu.make_async_copy(trans.at[:, :, pl.ds(first, 128)], raw, load_sem.at[0]),
        pltpu.make_async_copy(interp, weights, load_sem.at[1]),
        pltpu.make_async_copy(child, own, load_sem.at[2]),
        pltpu.make_async_copy(far, listed, load_sem.at[3]),
        pltpu.make_async_copy(blocks_in, blocks, load_sem.at[4]),
        pltpu.make_async_copy(slot_in, slot_parent, load_sem.at[5]),
        pltpu.make_async_copy(angle_in, angle, load_sem.at[6]),
    ]
    for copy in loads:
        copy.start()
    pl.semaphore_wait(barrier, len(peers) + 2)

    def halo(i):
        at = pl.ds(pl.multiple_of(i * rows, rows), rows)
        return [
            pltpu.make_async_remote_copy(
                child.at[at, pl.ds(256, 256)], before.at[at, :],
                halo_send.at[0, i], halo_recv.at[0, i], device_id={"dir": above},
            ),
            pltpu.make_async_remote_copy(
                child.at[at, pl.ds(0, 256)], after.at[at, :],
                halo_send.at[1, i], halo_recv.at[1, i], device_id={"dir": below},
            ),
        ]

    for i in range(CHUNKS):
        for copy in halo(i):
            copy.start()

    loads[6].wait()
    cosine[...] = jnp.cos(angle[...])
    sine[...] = jnp.sin(angle[...])
    loads[1].wait()
    loads[4].wait()
    for j in range(16):
        rel = [(blocks[b, j] - (dd * 4 + j // 4) + 18) & 15 for b in range(4)]
        for o in range(5):
            value = None
            for b in (o - 1, o):
                if 0 <= b < 4:
                    term = weights[j, b].astype(jnp.float32) * jnp.where(rel[b] == o, 1.0, 0.0)
                    value = term if value is None else value + term
            lanes = pl.ds((j % 4) * 128, 128)
            weight[j // 4, pl.ds(o * 128, 128), lanes] = value.astype(jnp.bfloat16)

    loads[3].wait()
    loads[5].wait()
    lane = lax.broadcasted_iota(jnp.int32, (189, 128), 1)
    for t in range(4):
        watch = listed[:, pl.ds((t + 1 if t < 3 else 2) * 128, 128)]
        occ[t : t + 1, :] = jnp.max(jnp.where(watch == lane + t * 128, 1.0, 0.0), axis=0, keepdims=True)
    ident = lax.broadcasted_iota(jnp.int32, (4, 128), 0) * 128 + lax.broadcasted_iota(jnp.int32, (4, 128), 1)
    for s in range(16):
        held = jnp.where(ident == slot_parent[bb * 16 + s], occ[...], 0.0)
        held = jnp.max(jnp.max(held, axis=1, keepdims=True), axis=0, keepdims=True)
        mask[s] = jnp.broadcast_to(held, (8, 128))

    def invert(i, found):
        return tuple(
            jnp.where(ident == slot_parent[i * 4 + k], i * 4 + k, found[k]) for k in range(4)
        )

    zero = jnp.zeros((4, 128), jnp.int32)
    found = lax.fori_loop(0, 128, invert, (zero,) * 4, unroll=4)
    slot_vec[...] = jnp.maximum(jnp.maximum(found[0], found[1]), jnp.maximum(found[2], found[3]))
    slot_copies = [
        pltpu.make_async_copy(slot_vec.at[t], slot_of.at[pl.ds(t * 128, 128)], load_sem.at[7 + t])
        for t in range(4)
    ]
    for copy in slot_copies:
        copy.start()

    loads[0].wait()
    for x in range(2, 5):
        for y in range(2, 5):
            for z in range(2, 5):
                raw[x * 49 + y * 7 + z] = jnp.zeros((2, 128), jnp.float32)

    def table_x(i, carry):
        t = [raw[x * 49 + i] for x in range(7)]
        vals = [t[1], t[3], t[5], t[2] - t[1], t[4] - t[3], t[6] - t[5]]
        vals += [t[0] - t[1], t[2] - t[3], t[4] - t[5]]
        for g, v in enumerate(vals):
            tab[i, g] = v
        return carry

    lax.fori_loop(0, 49, table_x, 0)

    def table_z(y, carry):
        def inner(g, carry):
            vals = line_kernel([tab[y * 7 + z, g] for z in range(7)])
            for fz, v in enumerate(vals):
                tab_z[y * F1 + fz, g] = v
            return carry

        return lax.fori_loop(0, 9, inner, carry, unroll=3)

    lax.fori_loop(0, 7, table_z, 0)

    def table_y(fz, carry):
        def inner(g, carry):
            vals = line_kernel([tab_z[y * F1 + fz, g] for y in range(7)])
            for fy, v in enumerate(vals):
                tab[fy * F1 + fz, g] = v
            return carry

        return lax.fori_loop(0, 9, inner, carry, unroll=3)

    lax.fori_loop(0, F1, table_y, 0)
    loads[2].wait()
    row = lax.broadcasted_iota(jnp.int32, (8, 128), 0)
    low = row < 4

    def chunk(i, carry):
        for copy in halo(i):
            copy.wait_recv()
        at = pl.ds(pl.multiple_of(i * rows, rows), rows)
        for c in range(4):
            parts = []
            if c < 2:
                parts.append((before, c * 128, (2 - c) * 128, 0))
            lo, hi = max(c, 2), min(c + 5, 6)
            parts.append((own, (lo - 2) * 128, (hi - lo) * 128, (lo - c) * 128))
            if c > 1:
                parts.append((after, 0, (c - 1) * 128, (6 - c) * 128))
            acc = None
            for ref, col, width, wrow in parts:
                piece = jnp.dot(
                    ref[at, pl.ds(col, width)],
                    weight[c, pl.ds(wrow, width), :],
                    preferred_element_type=jnp.float32,
                )
                acc = piece if acc is None else acc + piece
            total[c % 2] = acc

            def tile_of(tile, carry, c=c):
                lane = tile * 128
                wide = c * 512 + tile * 128
                re = im = None
                for h in range(8):
                    ur = total[c % 2, pl.ds(h * 16, 8), pl.ds(lane, 128)]
                    ui = total[c % 2, pl.ds(h * 16 + 8, 8), pl.ds(lane, 128)]
                    cs = jnp.broadcast_to(cosine[h : h + 1, pl.ds(wide, 128)], (8, 128))
                    sn = jnp.broadcast_to(sine[h : h + 1, pl.ds(wide, 128)], (8, 128))
                    r, m = cs * ur - sn * ui, sn * ur + cs * ui
                    re = r if re is None else re + r
                    im = m if im is None else im + m
                keep = mask[i]
                re, im = re * keep, im * keep
                stage[(c * 4 + tile) * 2, i] = jnp.where(low, re, pltpu.roll(im, 4, 0)).astype(jnp.bfloat16)
                stage[(c * 4 + tile) * 2 + 1, i] = jnp.where(low, pltpu.roll(re, 4, 0), im).astype(jnp.bfloat16)
                return carry

            for tile in range(4):
                tile_of(tile, 0)
        for peer in peers:
            pltpu.make_async_remote_copy(
                stage.at[peer, i], pats.at[bb * 16 + i], move_send, move_recv,
                device_id={"box": peer},
            ).start()
        return carry

    lax.fori_loop(0, CHUNKS, chunk, 0)
    mine = pltpu.make_async_copy(stage.at[bb], pats.at[pl.ds(bb * 16, 16)], local_sem)
    mine.start()
    pick = (row & 2) == 0

    def expand(fy, carry):
        def inner(fz, carry):
            for g in range(9):
                here, there = tab.at[fy * F1 + fz, g], tab.at[fy * F1 + fz + 9, g]
                two = []
                for part in range(2):
                    left = jnp.broadcast_to(here[part : part + 1, :], (8, 128))
                    right = jnp.broadcast_to(there[part : part + 1, :], (8, 128))
                    two.append(jnp.where(pick, left, right))
                tiles[fy * 9 + fz, g, 0] = two[0]
                tiles[fy * 9 + fz, g, 1] = jnp.where(low, -two[1], two[1])
            return carry

        return lax.fori_loop(0, 9, inner, carry)

    lax.fori_loop(0, F1, expand, 0)
    for copy in slot_copies:
        copy.wait()
    mine.wait()
    pltpu.make_async_copy(pats.at[pl.ds(0, 496)], pats.at[pl.ds(0, 496)], move_recv).wait()

    for half in range(2):

        def in_z(i, carry):
            vals = []
            for z in range(8):
                at = i * 8 + z
                if half == 0:
                    left, right = pats[slot_of[at]].astype(jnp.float32), pats[slot_of[at + 256]].astype(jnp.float32)
                    vals.append(jnp.where(pick, left, pltpu.roll(right, 2, 0)))
                    later[at] = jnp.where(pick, pltpu.roll(left, 6, 0), right)
                else:
                    vals.append(later[at])
            vals = line_in(vals)
            for fz in range(9):
                left, right = vals[fz], vals[fz + 9]
                lines[i * 9 + fz] = jnp.where(pick, left, pltpu.roll(right, 2, 0))
                lines[(i + 32) * 9 + fz] = jnp.where(pick, pltpu.roll(left, 6, 0), right)
            return carry

        lax.fori_loop(0, 32, in_z, 0, unroll=8)

        def in_y(x, carry):
            def inner(fz, carry):
                vals = line_in([lines[(x * 8 + y) * 9 + fz] for y in range(8)])
                for fy, v in enumerate(vals):
                    spec[fy * 9 + fz, x] = v
                return carry

            return lax.fori_loop(0, 9, inner, carry, unroll=9)

        lax.fori_loop(0, 8, in_y, 0)

        def product(f, carry):
            src = [spec[f, x] for x in range(8)]
            turn = [pltpu.roll(v, 4, 0) for v in src]
            sets = [
                ([src[2 * j] + src[2 * j + 1] for j in range(4)], [turn[2 * j] + turn[2 * j + 1] for j in range(4)]),
                (src[1::2], turn[1::2]),
                (src[0::2], turn[0::2]),
            ]
            sums = []
            for g, (x, t) in enumerate(sets):
                acc = [None] * 4
                for j in range(-1, 2):
                    a, b = tiles[f, g * 3 + j + 1, 0], tiles[f, g * 3 + j + 1, 1]
                    for i in range(4):
                        if 0 <= i + j < 4:
                            v = a * x[i + j] + b * t[i + j]
                            acc[i] = v if acc[i] is None else acc[i] + v
                sums.append(acc)
            for i in range(4):
                spec[f, 2 * i] = sums[0][i] + sums[1][i]
                spec[f, 2 * i + 1] = sums[0][i] + sums[2][i]
            return carry

        lax.fori_loop(0, NF // 2, product, 0, unroll=18)

        def out_y(x, carry):
            def inner(fz, carry):
                vals = line_out([spec[fy * 9 + fz, x] for fy in range(F1)])
                for y, v in enumerate(vals):
                    lines[(x * 8 + y) * 9 + fz] = v
                return carry

            return lax.fori_loop(0, 9, inner, carry, unroll=9)

        lax.fori_loop(0, 8, out_y, 0)

        def out_z(i, carry):
            near, away = [], []
            for fz in range(9):
                left, right = lines[i * 9 + fz], lines[(i + 32) * 9 + fz]
                near.append(jnp.where(pick, left, pltpu.roll(right, 2, 0)))
                away.append(jnp.where(pick, pltpu.roll(left, 6, 0), right))
            for z, v in enumerate(line_out(near + away)):
                grid_x[i * 8 + z] = v
                grid_x[256 + i * 8 + z] = pltpu.roll(v, 6, 0)
            return carry

        lax.fori_loop(0, 32, out_z, 0, unroll=8)

        def give(target, half=half):
            for q in range(4):
                vals = [grid_x[slot_parent[target * 16 + 4 * q + k]] for k in range(4)]
                pairs = [jnp.where(pick, vals[k], pltpu.roll(vals[k + 1], 2, 0)) for k in (0, 2)]
                back[half, target, q] = jnp.concatenate(pairs, axis=0).astype(jnp.bfloat16)

        for peer in peers:
            give(peer)
            pltpu.make_async_remote_copy(
                back.at[half, peer], out.at[half, bb], back_send.at[half], back_recv.at[half],
                device_id={"box": peer},
            ).start()
        give(bb)
        pltpu.make_async_copy(back.at[half, bb], out.at[half, bb], home_sem.at[half]).start()

    for i in range(CHUNKS):
        for copy in halo(i):
            copy.wait_send()
    most = pl.ds(0, 31)
    pltpu.make_async_copy(stage.at[most], stage.at[most], move_send).wait()
    for half in range(2):
        pltpu.make_async_copy(back.at[half, bb], out.at[half, bb], home_sem.at[half]).wait()
        sent, got = back.at[half, most], out.at[half, most]
        pltpu.make_async_copy(sent, sent, back_send.at[half]).wait()
        pltpu.make_async_copy(got, got, back_recv.at[half]).wait()


def far_pieces(child, interp, blocks, angle, slot_parent, far, trans):
    any_space = pl.BlockSpec(memory_space=pl.ANY)
    return pl.pallas_call(
        main_kernel,
        in_specs=[any_space] * 7,
        out_specs=any_space,
        out_shape=jax.ShapeDtypeStruct((2, 32, 4, 16, 128), jnp.bfloat16),
        scratch_shapes=[
            pltpu.VMEM((2048, 512), jnp.bfloat16),
            pltpu.VMEM((2048, 256), jnp.bfloat16),
            pltpu.VMEM((2048, 256), jnp.bfloat16),
            pltpu.VMEM((16, 4, 128, 128), jnp.bfloat16),
            pltpu.VMEM((4, 640, 512), jnp.bfloat16),
            pltpu.VMEM((2, 2048 // CHUNKS, 512), jnp.float32),
            pltpu.VMEM((32, 16, 8, 128), jnp.bfloat16),
            pltpu.VMEM((8, 2048), jnp.float32),
            pltpu.VMEM((8, 2048), jnp.float32),
            pltpu.VMEM((343, 2, 128), jnp.float32),
            pltpu.VMEM((7 * F1, 9, 2, 128), jnp.float32),
            pltpu.VMEM((NF, 9, 2, 128), jnp.float32),
            pltpu.VMEM((NF // 2, 9, 2, 8, 128), jnp.float32),
            pltpu.VMEM((189, 512), jnp.int32),
            pltpu.VMEM((4, 128), jnp.float32),
            pltpu.VMEM((16, 8, 128), jnp.float32),
            pltpu.VMEM((4, 128), jnp.int32),
            pltpu.SMEM((512,), jnp.int32),
            pltpu.SMEM((512,), jnp.int32),
            pltpu.SMEM((4, 16), jnp.int32),
            pltpu.VMEM((8, 2048), jnp.float32),
            pltpu.VMEM((512, 8, 128), jnp.bfloat16),
            pltpu.VMEM((256, 8, 128), jnp.float32),
            pltpu.VMEM((512, 8, 128), jnp.float32),
            pltpu.VMEM((32 * F1, 8, 128), jnp.float32),
            pltpu.VMEM((NF // 2, 8, 8, 128), jnp.float32),
            pltpu.VMEM((2, 32, 4, 16, 128), jnp.bfloat16),
            pltpu.SemaphoreType.DMA((11,)),
            pltpu.SemaphoreType.DMA((2, CHUNKS)),
            pltpu.SemaphoreType.DMA((2, CHUNKS)),
            pltpu.SemaphoreType.DMA,
            pltpu.SemaphoreType.DMA,
            pltpu.SemaphoreType.DMA,
            pltpu.SemaphoreType.DMA((2,)),
            pltpu.SemaphoreType.DMA((2,)),
            pltpu.SemaphoreType.DMA((2,)),
        ],
        compiler_params=pltpu.CompilerParams(collective_id=0, has_side_effects=True, vmem_limit_bytes=46 * 2**20),
    )(*[pltpu.with_memory_space_constraint(v, pltpu.HBM) for v in (child, interp, blocks, angle, slot_parent, far, trans)])


def arrange_kernel(src, dst, got, out, in_sem, out_sem):
    row = lax.broadcasted_iota(jnp.int32, (8, 128), 0)
    low, pick = row < 4, (row & 2) == 0

    def swap(a, b, mask, shift):
        return (
            jnp.where(mask, a, pltpu.roll(b, shift, 0)),
            jnp.where(mask, pltpu.roll(a, 8 - shift, 0), b),
        )

    fetch = [pltpu.make_async_copy(src.at[:, :, n], got.at[n], in_sem.at[n]) for n in range(4)]
    store = [pltpu.make_async_copy(out.at[pl.ds(4 * n, 4)], dst.at[pl.ds(4 * n, 4)], out_sem.at[n]) for n in range(4)]
    for copy in fetch:
        copy.start()
    for n in range(4):
        fetch[n].wait()
        for c in range(16):
            parts = [got[n, half, 2 * c + odd].astype(jnp.float32) for odd in range(2) for half in range(2)]
            lanes = slice(c * 128, c * 128 + 128)
            for k in range(2):
                v0, v1, v2, v3 = [v[8 * k : 8 * k + 8] for v in parts]
                p, r = swap(v0, v2, low, 4)
                q, s = swap(v1, v3, low, 4)
                at = 4 * n + 2 * k
                out[at, 0, :, lanes], out[at + 1, 0, :, lanes] = swap(p, q, pick, 2)
                out[at, 1, :, lanes], out[at + 1, 1, :, lanes] = swap(r, s, pick, 2)
        store[n].start()
    for copy in store:
        copy.wait()


def arrange(got):
    return pl.pallas_call(
        arrange_kernel,
        in_specs=[pl.BlockSpec(memory_space=pl.ANY)],
        out_specs=pl.BlockSpec(memory_space=pl.ANY),
        out_shape=jax.ShapeDtypeStruct((16, 2, 8, 2048), jnp.float32),
        scratch_shapes=[
            pltpu.VMEM((4, 2, 32, 16, 128), jnp.bfloat16),
            pltpu.VMEM((16, 2, 8, 2048), jnp.float32),
            pltpu.SemaphoreType.DMA((4,)),
            pltpu.SemaphoreType.DMA((4,)),
        ],
        compiler_params=pltpu.CompilerParams(vmem_limit_bytes=8 * 2**20),
    )(got)


def shards(child_pat, interp, interp_blocks, shift_angle, slot_parent, far_list, trans):
    pieces = far_pieces(
        child_pat.reshape(2048, 512),
        interp,
        interp_blocks.T,
        shift_angle,
        slot_parent,
        far_list.T,
        jnp.transpose(trans, (1, 0, 2)),
    )
    return arrange(pieces)


def solution(mesh):
    in_specs = (
        P("box", None, None, "dir"),
        P("dir", None, None, None),
        P("dir", None),
        P(None, "dir"),
        P(),
        P(),
        P(None, None, "dir"),
    )
    out_specs = P("box", None, None, "dir")
    return jax.shard_map(shards, mesh=mesh, in_specs=in_specs, out_specs=out_specs, check_vma=False)
```

```python
import jax
import jax.numpy as jnp
from jax import lax
from jax.experimental import pallas as pl
from jax.experimental.pallas import tpu as pltpu
from jax.sharding import PartitionSpec as P

G = 8
F1 = 18
NF = F1 * F1


def toom_in(v):
    a, b = v[0] + v[2], v[1] + v[3]
    c, d = v[0] + 4.0 * v[2], 2.0 * v[1] + 8.0 * v[3]
    return [v[0], v[3], a + b, a - b, c + d, c - d]


def line_in(x):
    even, odd = x[0::2], x[1::2]
    both = [e + o for e, o in zip(even, odd)]
    return toom_in(both) + toom_in(odd) + toom_in(even)


def toom_kernel(k):
    h2, h1, h0 = k
    a, b = (h0 + h2) * 0.5, h1 * 0.5
    c, d = (h0 + 4.0 * h2) * (1.0 / 24.0), h1 * (1.0 / 12.0)
    return [h0, h2, a + b, a - b, c + d, c - d]


def line_kernel(t):
    k0 = [t[1], t[3], t[5]]
    up = [t[2] - t[1], t[4] - t[3], t[6] - t[5]]
    down = [t[0] - t[1], t[2] - t[3], t[4] - t[5]]
    return toom_kernel(k0) + toom_kernel(up) + toom_kernel(down)


def toom_out(m):
    z0, z5 = m[0], m[1]
    e1, o1 = m[2] + m[3], m[2] - m[3]
    e2, d2 = m[4] + m[5], m[4] - m[5]
    z4 = e2 - e1 * (1.0 / 3.0) + z0 * 0.25
    z2 = e1 - z0 - z4
    z3 = 2.0 * d2 - o1 * (1.0 / 3.0) - 5.0 * z5
    z1 = o1 - z3 - z5
    return [z1, z2, z3, z4]


def line_out(m):
    base, up, down = toom_out(m[0:6]), toom_out(m[6:12]), toom_out(m[12:18])
    out = []
    for i in range(4):
        out += [base[i] + up[i], base[i] + down[i]]
    return out


TURNS = [(2, 2), (1, 2), (2, 1), (3, 2), (2, 3), (1, 1), (3, 1), (3, 3), (1, 3), (2, 0), (0, 2), (1, 0), (0, 1), (3, 0), (0, 3)]
PEERS = [(x, z, c) for x, z in TURNS for c in range(2)] + [(0, 0, 1)]
CHUNKS = 16


def peers_of(bb):
    x, z, c = bb // 8, (bb // 2) % 4, bb % 2
    return [((x + dx) % 4) * 8 + ((z + dz) % 4) * 2 + (c + dc) % 2 for dx, dz, dc in PEERS]


def main_kernel(
    child, interp, blocks_in, angle_in, slot_in, far, trans, out,
    own, before, after, weights, weight, total, stage, cosine, sine, raw, tab_z, tab, tiles,
    listed, occ, mask, slot_vec, slot_of, slot_parent, blocks, angle,
    pats, later, grid_x, lines, spec, back,
    load_sem, halo_send, halo_recv, move_send, move_recv, local_sem, home_sem, back_send, back_recv,
):
    bb, dd = lax.axis_index("box"), lax.axis_index("dir")
    dirs = lax.axis_size("dir")
    rows = 2048 // CHUNKS
    peers = peers_of(bb)
    above, below = (dd + 1) % dirs, (dd + dirs - 1) % dirs
    barrier = pltpu.get_barrier_semaphore()
    pl.semaphore_signal(barrier, 1, device_id={"dir": above})
    pl.semaphore_signal(barrier, 1, device_id={"dir": below})
    for peer in peers:
        pl.semaphore_signal(barrier, 1, device_id={"box": peer})
    first = pl.multiple_of((bb // 2) * 128, 128)
    loads = [
        pltpu.make_async_copy(trans.at[:, :, pl.ds(first, 128)], raw, load_sem.at[0]),
        pltpu.make_async_copy(interp, weights, load_sem.at[1]),
        pltpu.make_async_copy(child, own, load_sem.at[2]),
        pltpu.make_async_copy(far, listed, load_sem.at[3]),
        pltpu.make_async_copy(blocks_in, blocks, load_sem.at[4]),
        pltpu.make_async_copy(slot_in, slot_parent, load_sem.at[5]),
        pltpu.make_async_copy(angle_in, angle, load_sem.at[6]),
    ]
    pl.semaphore_wait(barrier, len(peers) + 2)

    def halo(i):
        at = pl.ds(pl.multiple_of(i * rows, rows), rows)
        return [
            pltpu.make_async_remote_copy(
                child.at[at, pl.ds(256, 256)], before.at[at, :],
                halo_send.at[0, i], halo_recv.at[0, i], device_id={"dir": above},
            ),
            pltpu.make_async_remote_copy(
                child.at[at, pl.ds(0, 256)], after.at[at, :],
                halo_send.at[1, i], halo_recv.at[1, i], device_id={"dir": below},
            ),
        ]

    for i in range(CHUNKS):
        for copy in halo(i):
            copy.start()
    for copy in loads:
        copy.start()

    loads[6].wait()
    cosine[...] = jnp.cos(angle[...])
    sine[...] = jnp.sin(angle[...])
    loads[1].wait()
    loads[4].wait()
    for j in range(16):
        rel = [(blocks[b, j] - (dd * 4 + j // 4) + 18) & 15 for b in range(4)]
        for o in range(5):
            value = None
            for b in (o - 1, o):
                if 0 <= b < 4:
                    term = weights[j, b].astype(jnp.float32) * jnp.where(rel[b] == o, 1.0, 0.0)
                    value = term if value is None else value + term
            lanes = pl.ds((j % 4) * 128, 128)
            weight[j // 4, pl.ds(o * 128, 128), lanes] = value.astype(jnp.bfloat16)

    loads[3].wait()
    loads[5].wait()
    lane = lax.broadcasted_iota(jnp.int32, (189, 128), 1)
    for t in range(4):
        watch = listed[:, pl.ds((t + 1 if t < 3 else 2) * 128, 128)]
        occ[t : t + 1, :] = jnp.max(jnp.where(watch == lane + t * 128, 1.0, 0.0), axis=0, keepdims=True)
    ident = lax.broadcasted_iota(jnp.int32, (4, 128), 0) * 128 + lax.broadcasted_iota(jnp.int32, (4, 128), 1)
    for s in range(16):
        held = jnp.where(ident == slot_parent[bb * 16 + s], occ[...], 0.0)
        held = jnp.max(jnp.max(held, axis=1, keepdims=True), axis=0, keepdims=True)
        mask[s] = jnp.broadcast_to(held, (8, 128))

    def invert(i, found):
        return tuple(
            jnp.where(ident == slot_parent[i * 4 + k], i * 4 + k, found[k]) for k in range(4)
        )

    zero = jnp.zeros((4, 128), jnp.int32)
    found = lax.fori_loop(0, 128, invert, (zero,) * 4, unroll=4)
    slot_vec[...] = jnp.maximum(jnp.maximum(found[0], found[1]), jnp.maximum(found[2], found[3]))
    slot_copies = [
        pltpu.make_async_copy(slot_vec.at[t], slot_of.at[pl.ds(t * 128, 128)], load_sem.at[7 + t])
        for t in range(4)
    ]
    for copy in slot_copies:
        copy.start()

    loads[0].wait()
    for x in range(2, 5):
        for y in range(2, 5):
            for z in range(2, 5):
                raw[x * 49 + y * 7 + z] = jnp.zeros((2, 128), jnp.float32)

    def table_x(i, carry):
        t = [raw[x * 49 + i] for x in range(7)]
        vals = [t[1], t[3], t[5], t[2] - t[1], t[4] - t[3], t[6] - t[5]]
        vals += [t[0] - t[1], t[2] - t[3], t[4] - t[5]]
        for g, v in enumerate(vals):
            tab[i, g] = v
        return carry

    lax.fori_loop(0, 49, table_x, 0)

    def table_z(y, carry):
        def inner(g, carry):
            vals = line_kernel([tab[y * 7 + z, g] for z in range(7)])
            for fz, v in enumerate(vals):
                tab_z[y * F1 + fz, g] = v
            return carry

        return lax.fori_loop(0, 9, inner, carry, unroll=3)

    lax.fori_loop(0, 7, table_z, 0)

    def table_y(fz, carry):
        def inner(g, carry):
            vals = line_kernel([tab_z[y * F1 + fz, g] for y in range(7)])
            for fy, v in enumerate(vals):
                tab[fy * F1 + fz, g] = v
            return carry

        return lax.fori_loop(0, 9, inner, carry, unroll=3)

    lax.fori_loop(0, F1, table_y, 0)
    loads[2].wait()
    row = lax.broadcasted_iota(jnp.int32, (8, 128), 0)
    low = row < 4

    def chunk(i, carry):
        for copy in halo(i):
            copy.wait_recv()
        at = pl.ds(pl.multiple_of(i * rows, rows), rows)
        for c in range(4):
            parts = []
            if c < 2:
                parts.append((before, c * 128, (2 - c) * 128, 0))
            lo, hi = max(c, 2), min(c + 5, 6)
            parts.append((own, (lo - 2) * 128, (hi - lo) * 128, (lo - c) * 128))
            if c > 1:
                parts.append((after, 0, (c - 1) * 128, (6 - c) * 128))
            acc = None
            for ref, col, width, wrow in parts:
                piece = jnp.dot(
                    ref[at, pl.ds(col, width)],
                    weight[c, pl.ds(wrow, width), :],
                    preferred_element_type=jnp.float32,
                )
                acc = piece if acc is None else acc + piece
            total[c % 2] = acc

            def tile_of(tile, carry, c=c):
                lane = tile * 128
                wide = c * 512 + tile * 128
                re = im = None
                for h in range(8):
                    ur = total[c % 2, pl.ds(h * 16, 8), pl.ds(lane, 128)]
                    ui = total[c % 2, pl.ds(h * 16 + 8, 8), pl.ds(lane, 128)]
                    cs = jnp.broadcast_to(cosine[h : h + 1, pl.ds(wide, 128)], (8, 128))
                    sn = jnp.broadcast_to(sine[h : h + 1, pl.ds(wide, 128)], (8, 128))
                    r, m = cs * ur - sn * ui, sn * ur + cs * ui
                    re = r if re is None else re + r
                    im = m if im is None else im + m
                keep = mask[i]
                re, im = re * keep, im * keep
                stage[(c * 4 + tile) * 2, i] = jnp.where(low, re, pltpu.roll(im, 4, 0)).astype(jnp.bfloat16)
                stage[(c * 4 + tile) * 2 + 1, i] = jnp.where(low, pltpu.roll(re, 4, 0), im).astype(jnp.bfloat16)
                return carry

            for tile in range(4):
                tile_of(tile, 0)
        for peer in peers:
            pltpu.make_async_remote_copy(
                stage.at[peer, i], pats.at[bb * 16 + i], move_send, move_recv,
                device_id={"box": peer},
            ).start()
        return carry

    lax.fori_loop(0, CHUNKS, chunk, 0)
    mine = pltpu.make_async_copy(stage.at[bb], pats.at[pl.ds(bb * 16, 16)], local_sem)
    mine.start()
    pick = (row & 2) == 0

    def expand(fy, carry):
        def inner(fz, carry):
            for g in range(9):
                here, there = tab.at[fy * F1 + fz, g], tab.at[fy * F1 + fz + 9, g]
                two = []
                for part in range(2):
                    left = jnp.broadcast_to(here[part : part + 1, :], (8, 128))
                    right = jnp.broadcast_to(there[part : part + 1, :], (8, 128))
                    two.append(jnp.where(pick, left, right))
                tiles[fy * 9 + fz, g, 0] = two[0]
                tiles[fy * 9 + fz, g, 1] = jnp.where(low, -two[1], two[1])
            return carry

        return lax.fori_loop(0, 9, inner, carry)

    lax.fori_loop(0, F1, expand, 0)
    for copy in slot_copies:
        copy.wait()
    mine.wait()
    pltpu.make_async_copy(pats.at[pl.ds(0, 496)], pats.at[pl.ds(0, 496)], move_recv).wait()

    for half in range(2):

        def in_z(i, carry):
            vals = []
            for z in range(8):
                at = i * 8 + z
                if half == 0:
                    left, right = pats[slot_of[at]].astype(jnp.float32), pats[slot_of[at + 256]].astype(jnp.float32)
                    vals.append(jnp.where(pick, left, pltpu.roll(right, 2, 0)))
                    later[at] = jnp.where(pick, pltpu.roll(left, 6, 0), right)
                else:
                    vals.append(later[at])
            vals = line_in(vals)
            for fz in range(9):
                left, right = vals[fz], vals[fz + 9]
                lines[i * 9 + fz] = jnp.where(pick, left, pltpu.roll(right, 2, 0))
                lines[(i + 32) * 9 + fz] = jnp.where(pick, pltpu.roll(left, 6, 0), right)
            return carry

        lax.fori_loop(0, 32, in_z, 0, unroll=8)

        def in_y(x, carry):
            def inner(fz, carry):
                vals = line_in([lines[(x * 8 + y) * 9 + fz] for y in range(8)])
                for fy, v in enumerate(vals):
                    spec[fy * 9 + fz, x] = v
                return carry

            return lax.fori_loop(0, 9, inner, carry, unroll=9)

        lax.fori_loop(0, 8, in_y, 0)

        def product(f, carry):
            src = [spec[f, x] for x in range(8)]
            turn = [pltpu.roll(v, 4, 0) for v in src]
            sets = [
                ([src[2 * j] + src[2 * j + 1] for j in range(4)], [turn[2 * j] + turn[2 * j + 1] for j in range(4)]),
                (src[1::2], turn[1::2]),
                (src[0::2], turn[0::2]),
            ]
            sums = []
            for g, (x, t) in enumerate(sets):
                acc = [None] * 4
                for j in range(-1, 2):
                    a, b = tiles[f, g * 3 + j + 1, 0], tiles[f, g * 3 + j + 1, 1]
                    for i in range(4):
                        if 0 <= i + j < 4:
                            v = a * x[i + j] + b * t[i + j]
                            acc[i] = v if acc[i] is None else acc[i] + v
                sums.append(acc)
            for i in range(4):
                spec[f, 2 * i] = sums[0][i] + sums[1][i]
                spec[f, 2 * i + 1] = sums[0][i] + sums[2][i]
            return carry

        lax.fori_loop(0, NF // 2, product, 0, unroll=18)

        def out_y(x, carry):
            def inner(fz, carry):
                vals = line_out([spec[fy * 9 + fz, x] for fy in range(F1)])
                for y, v in enumerate(vals):
                    lines[(x * 8 + y) * 9 + fz] = v
                return carry

            return lax.fori_loop(0, 9, inner, carry, unroll=9)

        lax.fori_loop(0, 8, out_y, 0)

        def out_z(i, carry):
            near, away = [], []
            for fz in range(9):
                left, right = lines[i * 9 + fz], lines[(i + 32) * 9 + fz]
                near.append(jnp.where(pick, left, pltpu.roll(right, 2, 0)))
                away.append(jnp.where(pick, pltpu.roll(left, 6, 0), right))
            for z, v in enumerate(line_out(near + away)):
                grid_x[i * 8 + z] = v
                grid_x[256 + i * 8 + z] = pltpu.roll(v, 6, 0)
            return carry

        lax.fori_loop(0, 32, out_z, 0, unroll=8)

        def give(target, half=half):
            for q in range(4):
                vals = [grid_x[slot_parent[target * 16 + 4 * q + k]] for k in range(4)]
                pairs = [jnp.where(pick, vals[k], pltpu.roll(vals[k + 1], 2, 0)) for k in (0, 2)]
                back[half, target, q] = jnp.concatenate(pairs, axis=0).astype(jnp.bfloat16)

        for peer in peers:
            give(peer)
            pltpu.make_async_remote_copy(
                back.at[half, peer], out.at[half, bb], back_send.at[half], back_recv.at[half],
                device_id={"box": peer},
            ).start()
        give(bb)
        pltpu.make_async_copy(back.at[half, bb], out.at[half, bb], home_sem.at[half]).start()

    for i in range(CHUNKS):
        for copy in halo(i):
            copy.wait_send()
    most = pl.ds(0, 31)
    pltpu.make_async_copy(stage.at[most], stage.at[most], move_send).wait()
    for half in range(2):
        pltpu.make_async_copy(back.at[half, bb], out.at[half, bb], home_sem.at[half]).wait()
        sent, got = back.at[half, most], out.at[half, most]
        pltpu.make_async_copy(sent, sent, back_send.at[half]).wait()
        pltpu.make_async_copy(got, got, back_recv.at[half]).wait()


def far_pieces(child, interp, blocks, angle, slot_parent, far, trans):
    any_space = pl.BlockSpec(memory_space=pl.ANY)
    return pl.pallas_call(
        main_kernel,
        in_specs=[any_space] * 7,
        out_specs=any_space,
        out_shape=jax.ShapeDtypeStruct((2, 32, 4, 16, 128), jnp.bfloat16),
        scratch_shapes=[
            pltpu.VMEM((2048, 512), jnp.bfloat16),
            pltpu.VMEM((2048, 256), jnp.bfloat16),
            pltpu.VMEM((2048, 256), jnp.bfloat16),
            pltpu.VMEM((16, 4, 128, 128), jnp.bfloat16),
            pltpu.VMEM((4, 640, 512), jnp.bfloat16),
            pltpu.VMEM((2, 2048 // CHUNKS, 512), jnp.float32),
            pltpu.VMEM((32, 16, 8, 128), jnp.bfloat16),
            pltpu.VMEM((8, 2048), jnp.float32),
            pltpu.VMEM((8, 2048), jnp.float32),
            pltpu.VMEM((343, 2, 128), jnp.float32),
            pltpu.VMEM((7 * F1, 9, 2, 128), jnp.float32),
            pltpu.VMEM((NF, 9, 2, 128), jnp.float32),
            pltpu.VMEM((NF // 2, 9, 2, 8, 128), jnp.float32),
            pltpu.VMEM((189, 512), jnp.int32),
            pltpu.VMEM((4, 128), jnp.float32),
            pltpu.VMEM((16, 8, 128), jnp.float32),
            pltpu.VMEM((4, 128), jnp.int32),
            pltpu.SMEM((512,), jnp.int32),
            pltpu.SMEM((512,), jnp.int32),
            pltpu.SMEM((4, 16), jnp.int32),
            pltpu.VMEM((8, 2048), jnp.float32),
            pltpu.VMEM((512, 8, 128), jnp.bfloat16),
            pltpu.VMEM((256, 8, 128), jnp.float32),
            pltpu.VMEM((512, 8, 128), jnp.float32),
            pltpu.VMEM((32 * F1, 8, 128), jnp.float32),
            pltpu.VMEM((NF // 2, 8, 8, 128), jnp.float32),
            pltpu.VMEM((2, 32, 4, 16, 128), jnp.bfloat16),
            pltpu.SemaphoreType.DMA((11,)),
            pltpu.SemaphoreType.DMA((2, CHUNKS)),
            pltpu.SemaphoreType.DMA((2, CHUNKS)),
            pltpu.SemaphoreType.DMA,
            pltpu.SemaphoreType.DMA,
            pltpu.SemaphoreType.DMA,
            pltpu.SemaphoreType.DMA((2,)),
            pltpu.SemaphoreType.DMA((2,)),
            pltpu.SemaphoreType.DMA((2,)),
        ],
        compiler_params=pltpu.CompilerParams(collective_id=0, has_side_effects=True, vmem_limit_bytes=46 * 2**20),
    )(*[pltpu.with_memory_space_constraint(v, pltpu.HBM) for v in (child, interp, blocks, angle, slot_parent, far, trans)])


def arrange_kernel(src, dst, got, out, in_sem, out_sem):
    row = lax.broadcasted_iota(jnp.int32, (8, 128), 0)
    low, pick = row < 4, (row & 2) == 0

    def swap(a, b, mask, shift):
        return (
            jnp.where(mask, a, pltpu.roll(b, shift, 0)),
            jnp.where(mask, pltpu.roll(a, 8 - shift, 0), b),
        )

    fetch = [pltpu.make_async_copy(src.at[:, :, n], got.at[n], in_sem.at[n]) for n in range(4)]
    store = [pltpu.make_async_copy(out.at[pl.ds(4 * n, 4)], dst.at[pl.ds(4 * n, 4)], out_sem.at[n]) for n in range(4)]
    for copy in fetch:
        copy.start()
    for n in range(4):
        fetch[n].wait()
        for c in range(16):
            parts = [got[n, half, 2 * c + odd].astype(jnp.float32) for odd in range(2) for half in range(2)]
            lanes = slice(c * 128, c * 128 + 128)
            for k in range(2):
                v0, v1, v2, v3 = [v[8 * k : 8 * k + 8] for v in parts]
                p, r = swap(v0, v2, low, 4)
                q, s = swap(v1, v3, low, 4)
                at = 4 * n + 2 * k
                out[at, 0, :, lanes], out[at + 1, 0, :, lanes] = swap(p, q, pick, 2)
                out[at, 1, :, lanes], out[at + 1, 1, :, lanes] = swap(r, s, pick, 2)
        store[n].start()
    for copy in store:
        copy.wait()


def arrange(got):
    return pl.pallas_call(
        arrange_kernel,
        in_specs=[pl.BlockSpec(memory_space=pl.ANY)],
        out_specs=pl.BlockSpec(memory_space=pl.ANY),
        out_shape=jax.ShapeDtypeStruct((16, 2, 8, 2048), jnp.float32),
        scratch_shapes=[
            pltpu.VMEM((4, 2, 32, 16, 128), jnp.bfloat16),
            pltpu.VMEM((16, 2, 8, 2048), jnp.float32),
            pltpu.SemaphoreType.DMA((4,)),
            pltpu.SemaphoreType.DMA((4,)),
        ],
        compiler_params=pltpu.CompilerParams(vmem_limit_bytes=8 * 2**20),
    )(got)


def shards(child_pat, interp, interp_blocks, shift_angle, slot_parent, far_list, trans):
    pieces = far_pieces(
        child_pat.reshape(2048, 512),
        interp,
        interp_blocks.T,
        shift_angle,
        slot_parent,
        far_list.T,
        jnp.transpose(trans, (1, 0, 2)),
    )
    return arrange(pieces)


def solution(mesh):
    in_specs = (
        P("box", None, None, "dir"),
        P("dir", None, None, None),
        P("dir", None),
        P(None, "dir"),
        P(),
        P(),
        P(None, None, "dir"),
    )
    out_specs = P("box", None, None, "dir")
    return jax.shard_map(shards, mesh=mesh, in_specs=in_specs, out_specs=out_specs, check_vma=False)
```
